512 devices in a mesh: wide: 64 (over z_hi, y, x, core), narrow: 8 (over z_lo).
Axes of the slice: x: 4, y: 4, z: 16 (z_hi: 2, z_lo: 8; z = z_hi * 8 + z_lo), core: 2. Of those that a mesh axis runs over, the one named last changes fastest.
Arguments:
- right_side: float32 [1024, 128, 128], P('wide', 'narrow'), may hold values from -8 to 8
- labels: int32 [128, 16, 16], P('wide', 'narrow'), may hold values from 0 to 15
- material_table: float32 [16], replicated, may hold values from 0.1 to 10
- robin_table: float32 [8], replicated, may hold values from 0.5 to 8
- robin_index: int32 [64, 8, 2], P('wide', 'narrow'), may hold values from 0 to 7
- coarse_rows: float32 [512, 512], P(('wide', 'narrow')), may hold values from -0.0014648438 to 0.0014648438
Outputs:
- solution: bfloat16 [1024, 128, 128], P('wide', 'narrow')
- residual: bfloat16 [1024, 128, 128], P('wide', 'narrow')
The draws below stay inside these ranges and needn't reach their ends.
All inputs are finite; a program needn't handle non-finite values.
Results may differ from the reference program's by a relative error of at most 0.0015.
Values sent between devices are 32-bit elements; how exact they have to be, the bound alone decides.
No kernel may reach another device: no remote copies, remote signals or barrier semaphores. Data moves between devices by JAX's collectives and lax.ppermute only.
A program may use at most 64 MiB of HBM per device.

```python
import math
import jax
import jax.numpy as jnp
from jax import lax

CX = 16
CY = 16
NZ = 128
BLOCK = 8
MATERIALS = 16
ROBINS = 8
SWEEPS = 4
ITERS = 2
NX = 1024
NY = 128
COARSE = 512
N_WIDE = 64
N_NARROW = 8


def place_ends(result, stream_key, low, largest):
    longest = result.shape.index(max(result.shape))
    spots = []
    for shift in (0, 1):
        where = [jax.random.randint(jax.random.fold_in(stream_key, axis), (), 0, length) for axis, length in enumerate(result.shape)]
        where[longest] = (where[longest] + shift) % result.shape[longest]
        spots.append(tuple(where))
    return result.at[spots[0]].set(low).at[spots[1]].set(largest)


def block_levels(rng, shape, split, least, top_value):
    gain = 1.0
    for dim, shards_of in split:
        heights = jax.random.uniform(jax.random.fold_in(jax.random.fold_in(rng, 6), dim), (shards_of,), jnp.float32, least / len(split), top_value / len(split))
        gain = gain * jnp.repeat(jnp.exp(heights), shape[dim] // shards_of).reshape((-1,) + (1,) * (len(shape) - 1 - dim))
    return gain


def scatter_about(stream_key, shape, deviation, bound, pieces=(), held_as=jnp.bfloat16):
    values = deviation * jax.random.normal(stream_key, shape, jnp.float32)
    if pieces:
        values = values * block_levels(stream_key, shape, pieces, -0.22, 0.18)
    return jnp.clip(values, -bound, bound).astype(held_as)


def setup_inputs(seed: int = 0) -> dict:
    key_of = jax.random.split(jax.random.key(seed), 7)
    return {
        "right_side": scatter_about(key_of[0], (NX, NY, NZ), 1.0, 8.0, ((0, 64), (1, 8)), jnp.float32),
        "labels": place_ends(jax.random.randint(key_of[1], (NX // BLOCK, NY // BLOCK, NZ // BLOCK), 0, MATERIALS), jax.random.fold_in(key_of[1], 1), 0, MATERIALS - 1).astype(jnp.int32),
        "material_table": jnp.clip(jnp.exp(jax.random.uniform(key_of[2], (MATERIALS,), jnp.float32, math.log(0.1), math.log(10.0))), 0.1, 10.0),
        "robin_table": jnp.clip(jnp.exp(jax.random.uniform(key_of[3], (ROBINS,), jnp.float32, math.log(0.5), math.log(8.0))), 0.5, 8.0),
        "robin_index": place_ends(jax.random.randint(key_of[4], (N_WIDE, N_NARROW, 2), 0, ROBINS), jax.random.fold_in(key_of[4], 1), 0, ROBINS - 1).astype(jnp.int32),
        "coarse_rows": scatter_about(key_of[5], (COARSE, COARSE), (COARSE * CX * CY * NZ) ** -0.5, 0.0014648438, ((0, 512),), jnp.float32),
    }


reaction = 1.0


def spread_cells(blocks):
    size_a, size_b, size_c = blocks.shape
    grown_up = jnp.broadcast_to(blocks[:, None, :, None, :, None], (size_a, BLOCK, size_b, BLOCK, size_c, BLOCK))
    return grown_up.reshape(size_a * BLOCK, size_b * BLOCK, size_c * BLOCK)


def spread_face(blocks):
    size_a, size_b = blocks.shape
    grown_up = jnp.broadcast_to(blocks[:, None, :, None], (size_a, BLOCK, size_b, BLOCK))
    return grown_up.reshape(size_a * BLOCK, size_b * BLOCK)


def face_conduct(kappa, west_k, east_k, south_k, north_k):
    west_v = jnp.concatenate([west_k[None], kappa[:-1]], 0)
    east_v = jnp.concatenate([kappa[1:], east_k[None]], 0)
    south_v = jnp.concatenate([south_k[:, None], kappa[:, :-1]], 1)
    north_v = jnp.concatenate([kappa[:, 1:], north_k[:, None]], 1)
    below_v = jnp.concatenate([kappa[:, :, :1], kappa[:, :, :-1]], 2)
    above_v = jnp.concatenate([kappa[:, :, 1:], kappa[:, :, -1:]], 2)
    return (0.5 * (kappa + west_v), 0.5 * (kappa + east_v), 0.5 * (kappa + south_v),
            0.5 * (kappa + north_v), 0.5 * (kappa + below_v), 0.5 * (kappa + above_v))


def neighbour_sum(field_now, conduct, borders):
    zero_layer = jnp.zeros_like(field_now[:, :, :1])
    coupled = conduct[0] * jnp.concatenate([borders[0][None], field_now[:-1]], 0)
    coupled = coupled + conduct[1] * jnp.concatenate([field_now[1:], borders[1][None]], 0)
    coupled = coupled + conduct[2] * jnp.concatenate([borders[2][:, None], field_now[:, :-1]], 1)
    coupled = coupled + conduct[3] * jnp.concatenate([field_now[:, 1:], borders[3][:, None]], 1)
    coupled = coupled + conduct[4] * jnp.concatenate([zero_layer, field_now[:, :, :-1]], 2)
    return coupled + conduct[5] * jnp.concatenate([field_now[:, :, 1:], zero_layer], 2)


def side_marks(shape):
    index_x = lax.broadcasted_iota(jnp.int32, (shape[0], shape[1], 1), 0)
    index_y = lax.broadcasted_iota(jnp.int32, (shape[0], shape[1], 1), 1)
    return ((index_x == 0).astype(jnp.float32), (index_x == shape[0] - 1).astype(jnp.float32),
            (index_y == 0).astype(jnp.float32), (index_y == shape[1] - 1).astype(jnp.float32))


def assemble_local(material):
    kappa_blocks, west_b, east_b, south_b, north_b, inside, robin_pair = material
    kappa = spread_cells(kappa_blocks)
    sides = (spread_face(west_b), spread_face(east_b), spread_face(south_b), spread_face(north_b))
    owned = (kappa[0], kappa[-1], kappa[:, 0], kappa[:, -1])
    chosen = [jnp.where(inside[side] > 0, sides[side], owned[side]) for side in range(4)]
    conduct = face_conduct(kappa, chosen[0], chosen[1], chosen[2], chosen[3])
    conduct_sum = conduct[0] + conduct[1] + conduct[2] + conduct[3] + conduct[4] + conduct[5]
    marks = side_marks(kappa.shape)
    robin_term = robin_pair[0] * (inside[0] * marks[0] + inside[1] * marks[1]) + robin_pair[1] * (inside[2] * marks[2] + inside[3] * marks[3])
    parity = (lax.broadcasted_iota(jnp.int32, kappa.shape, 0) + lax.broadcasted_iota(jnp.int32, kappa.shape, 1)
              + lax.broadcasted_iota(jnp.int32, kappa.shape, 2)) % 2
    return conduct, conduct_sum, robin_term, parity


def robin_source(traces, shape):
    marks = side_marks(shape)
    return (marks[0] * traces[0][None] + marks[1] * traces[1][None]
            + marks[2] * traces[2][:, None] + marks[3] * traces[3][:, None])


def relax(field_now, source, conduct, diagonal, parity):
    blank_x = jnp.zeros_like(field_now[0])
    blank_y = jnp.zeros_like(field_now[:, 0])
    blanks = (blank_x, blank_x, blank_y, blank_y)
    for sweep_at in range(SWEEPS):
        for colour in range(2):
            update = (source + neighbour_sum(field_now, conduct, blanks)) / diagonal
            field_now = jnp.where(parity == colour, update, field_now)
    return field_now


def misfit(field_now, source_part, conduct, conduct_sum, borders):
    return source_part - (reaction + conduct_sum) * field_now + neighbour_sum(field_now, conduct, borders)


def coarse_weights(extent_x, extent_y):
    along_x = (jnp.arange(extent_x, dtype=jnp.float32) + 0.5) / extent_x
    along_y = (jnp.arange(extent_y, dtype=jnp.float32) + 0.5) / extent_y
    return ((1.0 - along_x)[:, None] * (1.0 - along_y)[None, :], along_x[:, None] * (1.0 - along_y)[None, :],
            (1.0 - along_x)[:, None] * along_y[None, :], along_x[:, None] * along_y[None, :])


def restrict(leftover):
    column_sum = jnp.sum(leftover, axis=2)
    weights = coarse_weights(leftover.shape[0], leftover.shape[1])
    return jnp.stack([jnp.sum(weights[corner] * column_sum) for corner in range(4)])


def interpolate(corners, extent_x, extent_y):
    weights = coarse_weights(extent_x, extent_y)
    return corners[0, 0] * weights[0] + corners[1, 0] * weights[1] + corners[0, 1] * weights[2] + corners[1, 1] * weights[3]


def robin_traces(field_now, borders, conduct, inside, robin_pair):
    return (inside[0] * (conduct[0][0] * borders[0] + robin_pair[0] * field_now[0]),
            inside[1] * (conduct[1][-1] * borders[1] + robin_pair[0] * field_now[-1]),
            inside[2] * (conduct[2][:, 0] * borders[2] + robin_pair[1] * field_now[:, 0]),
            inside[3] * (conduct[3][:, -1] * borders[3] + robin_pair[1] * field_now[:, -1]))


def combine_partials(stacked):
    from_west = jnp.pad(stacked[:-1, :, 1], ((1, 0), (0, 0)))
    from_south = jnp.pad(stacked[:, :-1, 2], ((0, 0), (1, 0)))
    from_corner = jnp.pad(stacked[:-1, :-1, 3], ((1, 0), (1, 0)))
    return stacked[:, :, 0] + from_west + from_south + from_corner


def reference(right_side, labels, material_table, robin_table, robin_index, coarse_rows):
    blocks_total = N_WIDE * N_NARROW
    blocks_x, blocks_y, blocks_z = CX // BLOCK, CY // BLOCK, NZ // BLOCK

    def flat_blocks(array):
        return array.reshape((blocks_total,) + array.shape[2:])

    kappa_blocks = material_table[labels].reshape(N_WIDE, blocks_x, N_NARROW, blocks_y, blocks_z).transpose(0, 2, 1, 3, 4)
    west_b = jnp.concatenate([kappa_blocks[:1, :, 0], kappa_blocks[:-1, :, -1]], 0)
    east_b = jnp.concatenate([kappa_blocks[1:, :, 0], kappa_blocks[-1:, :, -1]], 0)
    south_b = jnp.concatenate([kappa_blocks[:, :1, :, 0], kappa_blocks[:, :-1, :, -1]], 1)
    north_b = jnp.concatenate([kappa_blocks[:, 1:, :, 0], kappa_blocks[:, -1:, :, -1]], 1)
    wide_pos = jnp.arange(N_WIDE)[:, None] + jnp.zeros((1, N_NARROW), jnp.int32)
    narrow_pos = jnp.arange(N_NARROW)[None, :] + jnp.zeros((N_WIDE, 1), jnp.int32)
    inside = jnp.stack([wide_pos > 0, wide_pos < N_WIDE - 1, narrow_pos > 0, narrow_pos < N_NARROW - 1], -1).astype(jnp.float32)
    robin_pair = robin_table[robin_index]
    material = tuple(flat_blocks(item) for item in (kappa_blocks, west_b, east_b, south_b, north_b, inside, robin_pair))
    source_blocks = flat_blocks(right_side.reshape(N_WIDE, CX, N_NARROW, CY, NZ).transpose(0, 2, 1, 3, 4))

    def outer_borders(solution_now):
        stacked = solution_now.reshape(N_WIDE, N_NARROW, CX, CY, NZ)
        zero_x = jnp.zeros_like(stacked[:1, :, 0])
        zero_y = jnp.zeros_like(stacked[:, :1, :, 0])
        west_f = jnp.concatenate([zero_x, stacked[:-1, :, -1]], 0)
        east_f = jnp.concatenate([stacked[1:, :, 0], zero_x], 0)
        south_f = jnp.concatenate([zero_y, stacked[:, :-1, :, -1]], 1)
        north_f = jnp.concatenate([stacked[:, 1:, :, 0], zero_y], 1)
        return tuple(flat_blocks(item) for item in (west_f, east_f, south_f, north_f))

    def sweep_block(packed):
        field_now, source_part, traces, local_mat = packed
        conduct, conduct_sum, robin_term, parity = assemble_local(local_mat)
        source = source_part + robin_source(traces, field_now.shape)
        diagonal = reaction + conduct_sum + robin_term
        return relax(field_now, source, conduct, diagonal, parity)

    def partial_block(packed):
        field_now, source_part, borders, local_mat = packed
        conduct, conduct_sum, robin_term, parity = assemble_local(local_mat)
        return restrict(misfit(field_now, source_part, conduct, conduct_sum, borders))

    def correct_block(packed):
        field_now, window = packed
        return field_now + interpolate(window[1:3, 1:3], CX, CY)[:, :, None]

    def trace_block(packed):
        field_now, borders, local_mat = packed
        conduct, conduct_sum, robin_term, parity = assemble_local(local_mat)
        return robin_traces(field_now, borders, conduct, local_mat[5], local_mat[6])

    def final_block(packed):
        field_now, source_part, borders, local_mat = packed
        conduct, conduct_sum, robin_term, parity = assemble_local(local_mat)
        return misfit(field_now, source_part, conduct, conduct_sum, borders)

    solution_now = jnp.zeros((blocks_total, CX, CY, NZ), jnp.float32)
    traces = (jnp.zeros((blocks_total, CY, NZ), jnp.float32), jnp.zeros((blocks_total, CY, NZ), jnp.float32),
              jnp.zeros((blocks_total, CX, NZ), jnp.float32), jnp.zeros((blocks_total, CX, NZ), jnp.float32))
    for outer in range(ITERS):
        solution_now = lax.map(sweep_block, (solution_now, source_blocks, traces, material))
        borders = outer_borders(solution_now)
        partials = lax.map(partial_block, (solution_now, source_blocks, borders, material))
        coarse_vec = combine_partials(partials.reshape(N_WIDE, N_NARROW, 4)).reshape(-1)
        coarse_all = jnp.dot(coarse_rows, coarse_vec, precision=lax.Precision.HIGHEST, preferred_element_type=jnp.float32)
        coarse_grid = jnp.pad(coarse_all.reshape(N_WIDE, N_NARROW), ((1, 2), (1, 2)))
        window_rows = [jnp.stack([coarse_grid[offset_x:offset_x + N_WIDE, offset_y:offset_y + N_NARROW] for offset_y in range(4)], -1)
                       for offset_x in range(4)]
        windows = flat_blocks(jnp.stack(window_rows, -2))
        solution_now = lax.map(correct_block, (solution_now, windows))
        borders = outer_borders(solution_now)
        if outer + 1 < ITERS:
            traces = lax.map(trace_block, (solution_now, borders, material))
    leftover = lax.map(final_block, (solution_now, source_blocks, borders, material))

    def to_grid(blocks):
        return blocks.reshape(N_WIDE, N_NARROW, CX, CY, NZ).transpose(0, 2, 1, 3, 4).reshape(NX, NY, NZ)

    return to_grid(solution_now).astype(jnp.bfloat16), to_grid(leftover).astype(jnp.bfloat16)
```

```python
import jax
import jax.numpy as jnp
from jax import lax
from jax.sharding import Mesh
from jax.sharding import PartitionSpec as P

BLOCK = 8
SWEEPS = 4
ITERS = 2


reaction = 1.0


def spread_cells(blocks):
    size_a, size_b, size_c = blocks.shape
    grown_up = jnp.broadcast_to(
        blocks[:, None, :, None, :, None], (size_a, BLOCK, size_b, BLOCK, size_c, BLOCK)
    )
    return grown_up.reshape(size_a * BLOCK, size_b * BLOCK, size_c * BLOCK)


def spread_face(blocks):
    size_a, size_b = blocks.shape
    grown_up = jnp.broadcast_to(blocks[:, None, :, None], (size_a, BLOCK, size_b, BLOCK))
    return grown_up.reshape(size_a * BLOCK, size_b * BLOCK)


def face_conduct(kappa, west_k, east_k, south_k, north_k):
    west_v = jnp.concatenate([west_k[None], kappa[:-1]], 0)
    east_v = jnp.concatenate([kappa[1:], east_k[None]], 0)
    south_v = jnp.concatenate([south_k[:, None], kappa[:, :-1]], 1)
    north_v = jnp.concatenate([kappa[:, 1:], north_k[:, None]], 1)
    below_v = jnp.concatenate([kappa[:, :, :1], kappa[:, :, :-1]], 2)
    above_v = jnp.concatenate([kappa[:, :, 1:], kappa[:, :, -1:]], 2)
    return (
        0.5 * (kappa + west_v),
        0.5 * (kappa + east_v),
        0.5 * (kappa + south_v),
        0.5 * (kappa + north_v),
        0.5 * (kappa + below_v),
        0.5 * (kappa + above_v),
    )


def neighbour_sum(field_now, conduct, borders):
    zero_layer = jnp.zeros_like(field_now[:, :, :1])
    coupled = conduct[0] * jnp.concatenate([borders[0][None], field_now[:-1]], 0)
    coupled = coupled + conduct[1] * jnp.concatenate([field_now[1:], borders[1][None]], 0)
    coupled = coupled + conduct[2] * jnp.concatenate([borders[2][:, None], field_now[:, :-1]], 1)
    coupled = coupled + conduct[3] * jnp.concatenate([field_now[:, 1:], borders[3][:, None]], 1)
    coupled = coupled + conduct[4] * jnp.concatenate([zero_layer, field_now[:, :, :-1]], 2)
    return coupled + conduct[5] * jnp.concatenate([field_now[:, :, 1:], zero_layer], 2)


def side_marks(shape):
    index_x = lax.broadcasted_iota(jnp.int32, (shape[0], shape[1], 1), 0)
    index_y = lax.broadcasted_iota(jnp.int32, (shape[0], shape[1], 1), 1)
    return (
        (index_x == 0).astype(jnp.float32),
        (index_x == shape[0] - 1).astype(jnp.float32),
        (index_y == 0).astype(jnp.float32),
        (index_y == shape[1] - 1).astype(jnp.float32),
    )


def assemble_local(material):
    kappa_blocks, west_b, east_b, south_b, north_b, inside, robin_pair = material
    kappa = spread_cells(kappa_blocks)
    sides = (spread_face(west_b), spread_face(east_b), spread_face(south_b), spread_face(north_b))
    owned = (kappa[0], kappa[-1], kappa[:, 0], kappa[:, -1])
    chosen = [jnp.where(inside[side] > 0, sides[side], owned[side]) for side in range(4)]
    conduct = face_conduct(kappa, chosen[0], chosen[1], chosen[2], chosen[3])
    conduct_sum = conduct[0] + conduct[1] + conduct[2] + conduct[3] + conduct[4] + conduct[5]
    marks = side_marks(kappa.shape)
    robin_term = robin_pair[0] * (inside[0] * marks[0] + inside[1] * marks[1]) + robin_pair[1] * (
        inside[2] * marks[2] + inside[3] * marks[3]
    )
    parity = (
        lax.broadcasted_iota(jnp.int32, kappa.shape, 0)
        + lax.broadcasted_iota(jnp.int32, kappa.shape, 1)
        + lax.broadcasted_iota(jnp.int32, kappa.shape, 2)
    ) % 2
    return (conduct, conduct_sum, robin_term, parity)


def robin_source(traces, shape):
    marks = side_marks(shape)
    return (
        marks[0] * traces[0][None]
        + marks[1] * traces[1][None]
        + marks[2] * traces[2][:, None]
        + marks[3] * traces[3][:, None]
    )


def relax(field_now, source, conduct, diagonal, parity):
    blank_x = jnp.zeros_like(field_now[0])
    blank_y = jnp.zeros_like(field_now[:, 0])
    blanks = (blank_x, blank_x, blank_y, blank_y)
    for sweep_at in range(SWEEPS):
        for colour in range(2):
            update = (source + neighbour_sum(field_now, conduct, blanks)) / diagonal
            field_now = jnp.where(parity == colour, update, field_now)
    return field_now


def misfit(field_now, source_part, conduct, conduct_sum, borders):
    return (
        source_part
        - (reaction + conduct_sum) * field_now
        + neighbour_sum(field_now, conduct, borders)
    )


def coarse_weights(extent_x, extent_y):
    along_x = (jnp.arange(extent_x, dtype=jnp.float32) + 0.5) / extent_x
    along_y = (jnp.arange(extent_y, dtype=jnp.float32) + 0.5) / extent_y
    return (
        (1.0 - along_x)[:, None] * (1.0 - along_y)[None, :],
        along_x[:, None] * (1.0 - along_y)[None, :],
        (1.0 - along_x)[:, None] * along_y[None, :],
        along_x[:, None] * along_y[None, :],
    )


def interpolate(corners, extent_x, extent_y):
    weights = coarse_weights(extent_x, extent_y)
    return (
        corners[0, 0] * weights[0]
        + corners[1, 0] * weights[1]
        + corners[0, 1] * weights[2]
        + corners[1, 1] * weights[3]
    )


def robin_traces(field_now, borders, conduct, inside, robin_pair):
    return (
        inside[0] * (conduct[0][0] * borders[0] + robin_pair[0] * field_now[0]),
        inside[1] * (conduct[1][-1] * borders[1] + robin_pair[0] * field_now[-1]),
        inside[2] * (conduct[2][:, 0] * borders[2] + robin_pair[1] * field_now[:, 0]),
        inside[3] * (conduct[3][:, -1] * borders[3] + robin_pair[1] * field_now[:, -1]),
    )


def table_lookup(keys, table):
    entries = jnp.arange(table.shape[0], dtype=jnp.int32)
    return jnp.sum(jnp.where(keys[..., None] == entries, table, 0.0), -1)


WIDE = ("half", "plane")
NEAR = 1.0 / 32.0
FAR = 31.0 / 32.0


def neighbour_pairs(peers, by):
    return [(i, i + by) for i in range(peers) if 0 <= i + by < peers]


def exchange(west, east, south, north, wide_count, narrow_count):
    return (
        lax.ppermute(east, WIDE, neighbour_pairs(wide_count, 1)),
        lax.ppermute(west, WIDE, neighbour_pairs(wide_count, -1)),
        lax.ppermute(north, "narrow", neighbour_pairs(narrow_count, 1)),
        lax.ppermute(south, "narrow", neighbour_pairs(narrow_count, -1)),
    )


def contributions(field_now, right_side, conduct, conduct_sum, inside):
    blank_x = jnp.zeros_like(field_now[0])
    blank_y = jnp.zeros_like(field_now[:, 0])
    own = misfit(field_now, right_side, conduct, conduct_sum, (blank_x, blank_x, blank_y, blank_y))
    ramp = (jnp.arange(16, dtype=jnp.float32) + 0.5) / 16
    pair = jnp.stack([1.0 - ramp, ramp])
    column_sum = jnp.sum(own, axis=2)
    centre = jnp.sum(pair[:, None, :, None] * pair[None, :, None, :] * column_sum, axis=(2, 3))
    west = inside[0] * jnp.sum(pair * jnp.sum(conduct[0][0] * field_now[0], -1), 1)
    east = inside[1] * jnp.sum(pair * jnp.sum(conduct[1][-1] * field_now[-1], -1), 1)
    south = inside[2] * jnp.sum(pair * jnp.sum(conduct[2][:, 0] * field_now[:, 0], -1), 1)
    north = inside[3] * jnp.sum(pair * jnp.sum(conduct[3][:, -1] * field_now[:, -1], -1), 1)
    centre = centre + FAR * (jnp.stack([west, east], 0) + jnp.stack([south, north], 1))
    zero = jnp.zeros((1,), jnp.float32)
    return jnp.concatenate(
        [
            zero, NEAR * west, zero,
            NEAR * south[:1], centre[0], NEAR * north[:1],
            NEAR * south[1:], centre[1], NEAR * north[1:],
            zero, NEAR * east, zero,
        ]
    )


def spread_rows(rows, wide_count, narrow_count, halves):
    grid = jnp.pad(rows.reshape(4, wide_count, narrow_count), ((0, 0), (1, 2), (1, 2)))
    moved = jnp.stack(
        [grid[:, i : i + wide_count, j : j + narrow_count] for i in range(4) for j in range(4)], -1
    )
    moved = moved.reshape(4, halves, wide_count // halves, narrow_count, 16)
    return moved.transpose(0, 1, 3, 2, 4).reshape(4, halves * narrow_count, -1)


def gather_all(values, planes, columns):
    first = lax.all_to_all(
        jnp.broadcast_to(values[None], (planes, 16)), "plane", 0, 0, tiled=True
    )
    second = jnp.broadcast_to(first.reshape(1, planes * 16), (columns, planes * 16))
    return lax.all_to_all(second, ("half", "narrow"), 0, 0, tiled=True)


def body(right_side, labels, material_table, robin_table, robin_index, coarse_rows):
    wide_at = lax.axis_index(WIDE)
    narrow_at = lax.axis_index("narrow")
    halves = lax.axis_size("half")
    planes = lax.axis_size("plane")
    wide_count = halves * planes
    narrow_count = lax.axis_size("narrow")
    extent_x, extent_y = (right_side.shape[0], right_side.shape[1])
    kappa_own = table_lookup(labels, material_table)
    flat = lambda item: item.reshape(1, -1)
    width = kappa_own[0].size
    from_west = lax.ppermute(flat(kappa_own[-1]), WIDE, neighbour_pairs(wide_count, 1))
    from_east = lax.ppermute(
        jnp.concatenate([flat(kappa_own[0]), coarse_rows], 1), WIDE, neighbour_pairs(wide_count, -1)
    )
    from_south = lax.ppermute(flat(kappa_own[:, -1]), "narrow", neighbour_pairs(narrow_count, 1))
    row_pair = jnp.concatenate([coarse_rows, from_east[:, width:]], 1)
    from_north = lax.ppermute(
        jnp.concatenate([flat(kappa_own[:, 0]), row_pair], 1),
        "narrow",
        neighbour_pairs(narrow_count, -1),
    )
    rows = jnp.concatenate([row_pair, from_north[:, width:]], 1)
    spread = spread_rows(rows, wide_count, narrow_count, halves)
    inside = jnp.stack(
        [wide_at > 0, wide_at < wide_count - 1, narrow_at > 0, narrow_at < narrow_count - 1]
    ).astype(jnp.float32)
    robin_pair = table_lookup(robin_index[0, 0], robin_table)
    material = (
        kappa_own,
        from_west.reshape(kappa_own[0].shape),
        from_east[:, :width].reshape(kappa_own[0].shape),
        from_south.reshape(kappa_own[:, 0].shape),
        from_north[:, :width].reshape(kappa_own[:, 0].shape),
        inside,
        robin_pair,
    )
    conduct, conduct_sum, robin_term, parity = assemble_local(material)
    diagonal = reaction + conduct_sum + robin_term
    solution_now = jnp.zeros_like(right_side)
    source = right_side
    for outer in range(ITERS):
        solution_now = relax(solution_now, source, conduct, diagonal, parity)
        every = gather_all(
            contributions(solution_now, right_side, conduct, conduct_sum, inside),
            planes,
            halves * narrow_count,
        )
        corners = jnp.sum(spread * every, axis=(1, 2)).reshape(2, 2).T
        solution_now = solution_now + interpolate(corners, extent_x, extent_y)[:, :, None]
        borders = exchange(
            solution_now[0], solution_now[-1], solution_now[:, 0], solution_now[:, -1], wide_count, narrow_count
        )
        if outer + 1 < ITERS:
            traces = robin_traces(solution_now, borders, conduct, inside, robin_pair)
            source = right_side + robin_source(traces, right_side.shape)
    leftover = misfit(solution_now, right_side, conduct, conduct_sum, borders)
    return (solution_now.astype(jnp.bfloat16), leftover.astype(jnp.bfloat16))


def solution(mesh):
    split = Mesh(mesh.devices.reshape(2, mesh.devices.shape[0] // 2, -1), ("half", "plane", "narrow"))
    placed = (
        P(WIDE, "narrow", None),
        P(WIDE, "narrow", None),
        P(),
        P(),
        P(WIDE, "narrow", None),
        P(("half", "plane", "narrow"), None),
    )
    return jax.shard_map(
        body,
        mesh=split,
        in_specs=placed,
        out_specs=(P(WIDE, "narrow", None), P(WIDE, "narrow", None)),
        check_vma=False,
    )
```

```python
import jax
import jax.numpy as jnp
from jax import lax
from jax.experimental import pallas as pl
from jax.experimental.pallas import tpu as pltpu
from jax.sharding import PartitionSpec as P

BLOCK = 8
SWEEPS = 4
CX = 16
CY = 16
NZ = 128
MATERIALS = 16
NEAR = 0.5 / 16
FAR = 15.5 / 16
INTERPRET = False
GRANT = 8 * 1024 * 1024
EXACT = lax.Precision.HIGHEST
F32 = jnp.float32
SHIFTS = [(i, j) for i in range(4) for j in range(4) if i in (1, 2) or j in (1, 2)]

VMEM = pl.BlockSpec(memory_space=pltpu.VMEM)
SMEM = pl.BlockSpec(memory_space=pltpu.SMEM)


def row_at(i):
    return (i + 0.5) / CX


def iota(shape, axis):
    return lax.broadcasted_iota(jnp.int32, shape, axis)


def rolled(value, shift, axis):
    return pltpu.roll(value, shift % value.shape[axis], axis)


def place():
    wide, narrow = lax.axis_index("wide"), lax.axis_index("narrow")
    last_wide, last_narrow = lax.axis_size("wide") - 1, lax.axis_size("narrow") - 1
    inside = tuple(
        jnp.where(flag, F32(1.0), F32(0.0))
        for flag in (wide > 0, wide < last_wide, narrow > 0, narrow < last_narrow)
    )
    return wide % 2 == 0, narrow % 2 == 0, inside


def sided(even, first, second):
    return jnp.where(even, second, first), jnp.where(even, first, second)


def eta_pair():
    eta = (iota((CY, NZ), 0).astype(F32) + 0.5) / CY
    return 1.0 - eta, eta


def robin_of(robin_index, robin_table):
    return robin_table[robin_index[0]], robin_table[robin_index[1]]


class Coefficients:
    def __init__(self, kap):
        row = lambda r: jnp.broadcast_to(kap[r : r + 1, :], (BLOCK, NZ))
        tile = lambda low, high: jnp.concatenate([row(low), row(high)], 0)
        at_y, at_z = iota((CY, NZ), 0), iota((CY, NZ), 1)
        both = (tile(0, 1), tile(2, 3))
        self.x = (
            [0.5 * (both[0] + tile(4, 5))]
            + [both[0]] * 7
            + [0.5 * (both[0] + both[1])]
            + [both[1]] * 7
            + [0.5 * (both[1] + tile(6, 7))]
        )
        self.south, self.north, self.below, self.above = [], [], [], []
        self.rest = []
        for a in range(2):
            k = both[a]
            flipped = tile(2 * a + 1, 2 * a)
            middle = 0.5 * (k + flipped)
            south = jnp.where(at_y == 0, 0.5 * (k + tile(8 + a, 8 + a)), jnp.where(at_y == BLOCK, middle, k))
            north = jnp.where(
                at_y == CY - 1, 0.5 * (k + tile(10 + a, 10 + a)), jnp.where(at_y == BLOCK - 1, middle, k)
            )
            below = jnp.where(at_z == 0, k, 0.5 * (k + rolled(k, 1, 1)))
            above = jnp.where(at_z == NZ - 1, k, 0.5 * (k + rolled(k, -1, 1)))
            self.south.append(south)
            self.north.append(north)
            self.rest.append(south + north + below + above)
            self.below.append(jnp.where(at_z == 0, 0.0, below))
            self.above.append(jnp.where(at_z == NZ - 1, 0.0, above))
        self.south_in = [jnp.where(at_y == 0, 0.0, c) for c in self.south]
        self.north_in = [jnp.where(at_y == CY - 1, 0.0, c) for c in self.north]
        self.at_y = at_y
        self.totals = {}

    def total(self, i):
        key = i if i in (0, 7, 8, 15) else i // BLOCK + 20
        if key not in self.totals:
            self.totals[key] = 1.0 + self.x[i] + self.x[i + 1] + self.rest[i // BLOCK]
        return self.totals[key]

    def coupling(self, u, i):
        a, here = i // BLOCK, u[i]
        total = self.south_in[a] * rolled(here, 1, 0) + self.north_in[a] * rolled(here, -1, 0)
        total = total + self.below[a] * rolled(here, 1, 1) + self.above[a] * rolled(here, -1, 1)
        if i > 0:
            total = total + self.x[i] * u[i - 1]
        if i < CX - 1:
            total = total + self.x[i + 1] * u[i + 1]
        return total


def relax(coef, inside, robin, u, source, first):
    at_y = coef.at_y
    side_y = robin[1] * (
        jnp.where(at_y == 0, inside[2], 0.0) + jnp.where(at_y == CY - 1, inside[3], 0.0)
    )
    inverse = {}
    for i in range(CX):
        key = i if i in (0, 7, 8, 15) else i // BLOCK + 20
        if key not in inverse:
            diagonal = coef.total(i) + side_y
            if i == 0:
                diagonal = diagonal + robin[0] * inside[0]
            if i == CX - 1:
                diagonal = diagonal + robin[0] * inside[1]
            inverse[key] = 1.0 / diagonal
        inverse[i + 100] = inverse[key]
    odd = (iota((CY, NZ), 0) + iota((CY, NZ), 1)) % 2
    masks = (odd == 0, odd == 1)
    for half in range(2 * SWEEPS):
        for i in range(CX):
            mask = masks[(i + half) % 2]
            if first and half == 0:
                u[i] = jnp.where(mask, source[i] * inverse[i + 100], 0.0)
            else:
                update = (source[i] + coef.coupling(u, i)) * inverse[i + 100]
                u[i] = jnp.where(mask, update, u[i])


def contribute(coef, inside, u, right, sums, out):
    weights = eta_pair()
    zero = jnp.zeros((CY, NZ), F32)
    own, south, north = [zero, zero], [zero, zero], [zero, zero]
    for i in range(CX):
        a, here = i // BLOCK, u[i]
        left = right[i] - coef.total(i) * here + coef.coupling(u, i)
        low, high = coef.south[a] * here, coef.north[a] * here
        for side, weight in enumerate((1.0 - row_at(i), row_at(i))):
            own[side] = own[side] + weight * left
            south[side] = south[side] + weight * low
            north[side] = north[side] + weight * high
    across = lambda value, b: jnp.sum(value * weights[b], axis=0, keepdims=True)
    west, east = inside[0] * coef.x[0] * u[0], inside[1] * coef.x[CX] * u[CX - 1]
    west_row = [across(west, b) for b in range(2)]
    east_row = [across(east, b) for b in range(2)]
    south_row = [inside[2] * south[a][:1] for a in range(2)]
    north_row = [inside[3] * north[a][CY - 1 :] for a in range(2)]
    sums[...] = jnp.zeros_like(sums)
    for a in range(2):
        for b in range(2):
            near_x, near_y = (west_row, east_row)[a][b], (south_row, north_row)[b][a]
            at = (1 + a) * 4 + 1 + b
            sums[at : at + 1, :] = across(own[a], b) + FAR * (near_x + near_y)
    for b in range(2):
        sums[1 + b : 2 + b, :] = NEAR * west_row[b]
        sums[13 + b : 14 + b, :] = NEAR * east_row[b]
    for a in range(2):
        at = (1 + a) * 4
        sums[at : at + 1, :] = NEAR * south_row[a]
        sums[at + 3 : at + 4, :] = NEAR * north_row[a]
    column = jnp.sum(sums[...], axis=1, keepdims=True)
    spread = jnp.where(iota((16, NZ), 0) == iota((16, NZ), 1), column, 0.0)
    out[...] = jnp.broadcast_to(jnp.sum(spread, axis=0, keepdims=True), out.shape)


def pack_kernel(labels, row, pay):
    pay[...] = jnp.zeros_like(pay)
    for a in range(2):
        pay[2 * a : 2 * a + 2, 0 : labels.shape[2]] = labels[a].astype(F32)
    for c in range(row.shape[1] // NZ):
        pay[4 + c : 5 + c, :] = row[:, c * NZ : (c + 1) * NZ]


def first_kernel(right, table, robin_table, robin_index, own, y2, y1, x1, x2, u, out, kap, east, sums):
    even_x, even_y, inside = place()
    from_west, from_east = sided(even_x, x1[...], x2[...])
    from_south, from_north = sided(even_y, y1[...], y2[...])
    east[...] = from_east
    keys = jnp.concatenate([own[...], from_west, from_east, from_south, from_north], 0)
    pick = (iota((NZ, NZ), 0) == iota((NZ, NZ), 1) // BLOCK).astype(F32)
    keys = jnp.dot(keys, pick, precision=EXACT, preferred_element_type=F32)
    found = jnp.zeros_like(keys)
    for m in range(MATERIALS):
        found = jnp.where(jnp.abs(keys - m) < 0.5, table[m], found)
    kap[...] = jnp.zeros_like(kap)
    kap[0:4, :] = found[0:4]
    for b in range(2):
        own_of = lambda a, c: found[2 * a + c : 2 * a + c + 1]
        kap[4 + b : 5 + b, :] = jnp.where(inside[0] > 0, found[10 + b : 11 + b], own_of(0, b))
        kap[6 + b : 7 + b, :] = jnp.where(inside[1] > 0, found[16 + b : 17 + b], own_of(1, b))
        kap[8 + b : 9 + b, :] = jnp.where(inside[2] > 0, found[25 + 2 * b : 26 + 2 * b], own_of(b, 0))
        kap[10 + b : 11 + b, :] = jnp.where(inside[3] > 0, found[32 + 2 * b : 33 + 2 * b], own_of(b, 1))
    coef = Coefficients(kap)
    relax(coef, inside, robin_of(robin_index, robin_table), u, right, True)
    contribute(coef, inside, u, right, sums, out)


def correct(every, own, east, north, corner, u, shifted, rows, new, sends):
    even_x, even_y, _ = place()
    count = rows.shape[1]
    narrow_count = lax.axis_size("narrow")
    wide_count = count // narrow_count
    rows[...] = jnp.zeros_like(rows)
    for k, pay in enumerate((own, east, north, corner)):
        for c in range(count // NZ):
            rows[k : k + 1, c * NZ : (c + 1) * NZ] = pay[4 + c : 5 + c, :]
    at = iota((8, count), 1)
    at_x, at_y = at // narrow_count, at % narrow_count
    held = rows[...]
    for t, (i, j) in enumerate(SHIFTS):
        x, y = at_x + (i - 1), at_y + (j - 1)
        fits = (x >= 0) & (x < wide_count) & (y >= 0) & (y < narrow_count)
        moved = rolled(held, -((i - 1) * narrow_count + j - 1), 1)
        shifted[8 * t : 8 * t + 8, :] = jnp.where(fits, moved, 0.0)
    product = jnp.dot(shifted[...], every[...], precision=EXACT, preferred_element_type=F32)
    lane = iota((8, NZ), 1)
    picked = jnp.zeros((8, NZ), F32)
    for t, (i, j) in enumerate(SHIFTS):
        picked = picked + jnp.where(lane == 4 * i + j, product[8 * t : 8 * t + 8], 0.0)
    value = jnp.sum(picked, axis=1, keepdims=True)
    value = [jnp.broadcast_to(value[k : k + 1], (CY, NZ)) for k in range(4)]
    low, high = eta_pair()
    west, east_side = value[0] * low + value[2] * high, value[1] * low + value[3] * high
    sx1, sx2, sy1, sy2 = sends
    for i in range(CX):
        now = u[i] + ((1.0 - row_at(i)) * west + row_at(i) * east_side)
        new[i] = now
        south, north_row = now[:1], now[CY - 1 :]
        sy1[i : i + 1, :] = jnp.where(even_y, north_row, south)
        sy2[i : i + 1, :] = jnp.where(even_y, south, north_row)
        if i == 0:
            first = now
    sx1[...] = jnp.where(even_x, now, first)
    sx2[...] = jnp.where(even_x, first, now)


def make_correct(final):
    def kernel(every, own, east, y1, y2, corner, u, new, sx1, sx2, sy1, sy2, *more):
        if final:
            solution_out, shifted, rows, north = more
        else:
            shifted, rows, north = more
        _, even_y, _ = place()
        north[...] = sided(even_y, y1[...], y2[...])[1]
        correct(every, own, east, north, corner, u, shifted, rows, new, (sx1, sx2, sy1, sy2))
        if final:
            solution_out[...] = new[...].astype(jnp.bfloat16)

    return kernel


def second_kernel(right, robin_table, robin_index, kap, old, x2, x1, y1, y2, u, out, source, sums):
    even_x, even_y, inside = place()
    west, east = sided(even_x, x1[...], x2[...])
    south, north = sided(even_y, y1[...], y2[...])
    robin = robin_of(robin_index, robin_table)
    coef = Coefficients(kap)
    for i in range(CX):
        a, here = i // BLOCK, old[i]
        u[i] = here
        total = right[i]
        trace = inside[2] * (coef.south[a] * south[i : i + 1] + robin[1] * here)
        total = total + jnp.where(coef.at_y == 0, trace, 0.0)
        trace = inside[3] * (coef.north[a] * north[i : i + 1] + robin[1] * here)
        total = total + jnp.where(coef.at_y == CY - 1, trace, 0.0)
        if i == 0:
            total = total + inside[0] * (coef.x[0] * west + robin[0] * here)
        if i == CX - 1:
            total = total + inside[1] * (coef.x[CX] * east + robin[0] * here)
        source[i] = total
    relax(coef, inside, robin, u, source, False)
    contribute(coef, inside, u, right, sums, out)


def last_kernel(right, kap, u, x2, x1, y1, y2, out):
    even_x, even_y, inside = place()
    west, east = sided(even_x, x1[...], x2[...])
    south, north = sided(even_y, y1[...], y2[...])
    coef = Coefficients(kap)
    for i in range(CX):
        a = i // BLOCK
        left = right[i] - coef.total(i) * u[i] + coef.coupling(u, i)
        left = left + jnp.where(coef.at_y == 0, inside[2] * coef.south[a] * south[i : i + 1], 0.0)
        left = left + jnp.where(coef.at_y == CY - 1, inside[3] * coef.north[a] * north[i : i + 1], 0.0)
        if i == 0:
            left = left + inside[0] * coef.x[0] * west
        if i == CX - 1:
            left = left + inside[1] * coef.x[CX] * east
        out[i] = left.astype(jnp.bfloat16)


def call(kernel, out_shape, spaces, scratch=()):
    return pl.pallas_call(
        kernel,
        out_shape=out_shape,
        in_specs=list(spaces),
        out_specs=jax.tree.map(lambda _: VMEM, out_shape),
        scratch_shapes=list(scratch),
        interpret=INTERPRET,
        compiler_params=pltpu.CompilerParams(vmem_limit_bytes=GRANT),
    )


def swap_pairs(peers, start):
    pairs = []
    for i in range(start, peers - 1, 2):
        pairs += [(i, i + 1), (i + 1, i)]
    return pairs


def swaps(sx1, sx2, sy1, sy2):
    wide_count, narrow_count = lax.axis_size("wide"), lax.axis_size("narrow")
    x2 = lax.ppermute(sx2, "wide", swap_pairs(wide_count, 1))
    x1 = lax.ppermute(sx1, "wide", swap_pairs(wide_count, 0))
    y1 = lax.ppermute(sy1, "narrow", swap_pairs(narrow_count, 0))
    y2 = lax.ppermute(sy2, "narrow", swap_pairs(narrow_count, 1))
    return x2, x1, y1, y2


def everywhere(values):
    return lax.all_to_all(values, ("wide", "narrow"), 0, 0, tiled=True)


def body(right_side, labels, material_table, robin_table, robin_index, coarse_rows):
    count = coarse_rows.shape[1]
    shape = lambda *dims: jax.ShapeDtypeStruct(dims, F32)
    field, face, gathered = shape(CX, CY, NZ), shape(CY, NZ), shape(count, NZ)
    pay_shape = shape(8, NZ)
    index = robin_index[0, 0]
    pay = call(pack_kernel, pay_shape, [VMEM] * 2)(labels, coarse_rows)
    x2, x1, y1, y2 = swaps(pay, pay, pay, pay)
    u, sent, kap, east = call(
        first_kernel,
        (field, gathered, shape(16, NZ), pay_shape),
        [VMEM] + [SMEM] * 3 + [VMEM] * 5,
        [pltpu.VMEM((16, NZ), F32)],
    )(right_side, material_table, robin_table, index, pay, y2, y1, x1, x2)
    narrow_count = lax.axis_size("narrow")
    corner = lax.ppermute(east, "narrow", [(i + 1, i) for i in range(narrow_count - 1)])
    work = [pltpu.VMEM((8 * len(SHIFTS), count), F32), pltpu.VMEM((8, count), F32), pltpu.VMEM((8, NZ), F32)]
    u, *faces = call(make_correct(False), (field, face, face, face, face), [VMEM] * 7, work)(
        everywhere(sent), pay, east, y1, y2, corner, u
    )
    seen = swaps(*faces)
    u, sent = call(
        second_kernel,
        (field, gathered),
        [VMEM] + [SMEM] * 2 + [VMEM] * 6,
        [pltpu.VMEM((CX, CY, NZ), F32), pltpu.VMEM((16, NZ), F32)],
    )(right_side, robin_table, index, kap, u, *seen)
    half = jax.ShapeDtypeStruct((CX, CY, NZ), jnp.bfloat16)
    u, f1, f2, f3, f4, answer = call(
        make_correct(True), (field, face, face, face, face, half), [VMEM] * 7, work
    )(everywhere(sent), pay, east, y1, y2, corner, u)
    seen = swaps(f1, f2, f3, f4)
    leftover = call(last_kernel, half, [VMEM] * 7)(right_side, kap, u, *seen)
    return (answer, leftover)


def solution(mesh):
    placed = (
        P("wide", "narrow", None),
        P("wide", "narrow", None),
        P(),
        P(),
        P("wide", "narrow", None),
        P(("wide", "narrow"), None),
    )
    return jax.shard_map(
        body,
        mesh=mesh,
        in_specs=placed,
        out_specs=(P("wide", "narrow", None), P("wide", "narrow", None)),
        check_vma=False,
    )
```

```python
import jax
import jax.numpy as jnp
from jax import lax
from jax.experimental import pallas as pl
from jax.experimental.pallas import tpu as pltpu
from jax.sharding import PartitionSpec as P


BLOCK = 8
SWEEPS = 4
CX = 16
CY = 16
NZ = 128
MATERIALS = 16
NEAR = 0.5 / 16
FAR = 15.5 / 16
INTERPRET = False
GRANT = 8 * 1024 * 1024
EXACT = lax.Precision.HIGHEST
F32 = jnp.float32
SHIFTS = [(i, j) for i in range(4) for j in range(4) if i in (1, 2) or j in (1, 2)]

VMEM = pl.BlockSpec(memory_space=pltpu.VMEM)
SMEM = pl.BlockSpec(memory_space=pltpu.SMEM)


def row_at(i):
    return (i + 0.5) / CX


def iota(shape, axis):
    return lax.broadcasted_iota(jnp.int32, shape, axis)


def rolled(value, shift, axis):
    return pltpu.roll(value, shift % value.shape[axis], axis)


def place():
    wide, narrow = lax.axis_index("wide"), lax.axis_index("narrow")
    last_wide, last_narrow = lax.axis_size("wide") - 1, lax.axis_size("narrow") - 1
    inside = tuple(
        jnp.where(flag, F32(1.0), F32(0.0))
        for flag in (wide > 0, wide < last_wide, narrow > 0, narrow < last_narrow)
    )
    return wide % 2 == 0, narrow % 2 == 0, inside


def sided(even, first, second):
    return jnp.where(even, second, first), jnp.where(even, first, second)


def eta_pair():
    eta = (iota((CY, NZ), 0).astype(F32) + 0.5) / CY
    return 1.0 - eta, eta


def robin_of(robin_index, robin_table):
    return robin_table[robin_index[0]], robin_table[robin_index[1]]


class Coefficients:
    def __init__(self, kap):
        row = lambda r: jnp.broadcast_to(kap[r : r + 1, :], (BLOCK, NZ))
        tile = lambda low, high: jnp.concatenate([row(low), row(high)], 0)
        at_y, at_z = iota((CY, NZ), 0), iota((CY, NZ), 1)
        both = (tile(0, 1), tile(2, 3))
        self.x = (
            [0.5 * (both[0] + tile(4, 5))]
            + [both[0]] * 7
            + [0.5 * (both[0] + both[1])]
            + [both[1]] * 7
            + [0.5 * (both[1] + tile(6, 7))]
        )
        self.south, self.north, self.below, self.above = [], [], [], []
        self.rest = []
        for a in range(2):
            k = both[a]
            flipped = tile(2 * a + 1, 2 * a)
            middle = 0.5 * (k + flipped)
            south = jnp.where(at_y == 0, 0.5 * (k + tile(8 + a, 8 + a)), jnp.where(at_y == BLOCK, middle, k))
            north = jnp.where(
                at_y == CY - 1, 0.5 * (k + tile(10 + a, 10 + a)), jnp.where(at_y == BLOCK - 1, middle, k)
            )
            below = jnp.where(at_z == 0, k, 0.5 * (k + rolled(k, 1, 1)))
            above = jnp.where(at_z == NZ - 1, k, 0.5 * (k + rolled(k, -1, 1)))
            self.south.append(south)
            self.north.append(north)
            self.rest.append(south + north + below + above)
            self.below.append(jnp.where(at_z == 0, 0.0, below))
            self.above.append(jnp.where(at_z == NZ - 1, 0.0, above))
        self.south_in = [jnp.where(at_y == 0, 0.0, c) for c in self.south]
        self.north_in = [jnp.where(at_y == CY - 1, 0.0, c) for c in self.north]
        self.at_y = at_y
        self.totals = {}

    def total(self, i):
        key = i if i in (0, 7, 8, 15) else i // BLOCK + 20
        if key not in self.totals:
            self.totals[key] = 1.0 + self.x[i] + self.x[i + 1] + self.rest[i // BLOCK]
        return self.totals[key]

    def coupling(self, u, i):
        a, here = i // BLOCK, u[i]
        total = self.south_in[a] * rolled(here, 1, 0) + self.north_in[a] * rolled(here, -1, 0)
        total = total + self.below[a] * rolled(here, 1, 1) + self.above[a] * rolled(here, -1, 1)
        if i > 0:
            total = total + self.x[i] * u[i - 1]
        if i < CX - 1:
            total = total + self.x[i + 1] * u[i + 1]
        return total


def relax(coef, inside, robin, u, source, first):
    at_y = coef.at_y
    side_y = robin[1] * (
        jnp.where(at_y == 0, inside[2], 0.0) + jnp.where(at_y == CY - 1, inside[3], 0.0)
    )
    inverse = {}
    for i in range(CX):
        key = i if i in (0, 7, 8, 15) else i // BLOCK + 20
        if key not in inverse:
            diagonal = coef.total(i) + side_y
            if i == 0:
                diagonal = diagonal + robin[0] * inside[0]
            if i == CX - 1:
                diagonal = diagonal + robin[0] * inside[1]
            inverse[key] = 1.0 / diagonal
        inverse[i + 100] = inverse[key]
    odd = (iota((CY, NZ), 0) + iota((CY, NZ), 1)) % 2
    masks = (odd == 0, odd == 1)
    for half in range(2 * SWEEPS):
        for i in range(CX):
            mask = masks[(i + half) % 2]
            if first and half == 0:
                u[i] = jnp.where(mask, source[i] * inverse[i + 100], 0.0)
            else:
                update = (source[i] + coef.coupling(u, i)) * inverse[i + 100]
                u[i] = jnp.where(mask, update, u[i])


def contribute(coef, inside, u, right, sums, out):
    weights = eta_pair()
    zero = jnp.zeros((CY, NZ), F32)
    own, south, north = [zero, zero], [zero, zero], [zero, zero]
    for i in range(CX):
        a, here = i // BLOCK, u[i]
        left = right[i] - coef.total(i) * here + coef.coupling(u, i)
        low, high = coef.south[a] * here, coef.north[a] * here
        for side, weight in enumerate((1.0 - row_at(i), row_at(i))):
            own[side] = own[side] + weight * left
            south[side] = south[side] + weight * low
            north[side] = north[side] + weight * high
    across = lambda value, b: jnp.sum(value * weights[b], axis=0, keepdims=True)
    west, east = inside[0] * coef.x[0] * u[0], inside[1] * coef.x[CX] * u[CX - 1]
    west_row = [across(west, b) for b in range(2)]
    east_row = [across(east, b) for b in range(2)]
    south_row = [inside[2] * south[a][:1] for a in range(2)]
    north_row = [inside[3] * north[a][CY - 1 :] for a in range(2)]
    sums[...] = jnp.zeros_like(sums)
    for a in range(2):
        for b in range(2):
            near_x, near_y = (west_row, east_row)[a][b], (south_row, north_row)[b][a]
            at = (1 + a) * 4 + 1 + b
            sums[at : at + 1, :] = across(own[a], b) + FAR * (near_x + near_y)
    for b in range(2):
        sums[1 + b : 2 + b, :] = NEAR * west_row[b]
        sums[13 + b : 14 + b, :] = NEAR * east_row[b]
    for a in range(2):
        at = (1 + a) * 4
        sums[at : at + 1, :] = NEAR * south_row[a]
        sums[at + 3 : at + 4, :] = NEAR * north_row[a]
    column = jnp.sum(sums[...], axis=1, keepdims=True)
    spread = jnp.where(iota((16, NZ), 0) == iota((16, NZ), 1), column, 0.0)
    out[...] = jnp.broadcast_to(jnp.sum(spread, axis=0, keepdims=True), out.shape)


def pack_kernel(labels, row, pay):
    pay[...] = jnp.zeros_like(pay)
    for a in range(2):
        pay[2 * a : 2 * a + 2, 0 : labels.shape[2]] = labels[a].astype(F32)
    for c in range(row.shape[1] // NZ):
        pay[4 + c : 5 + c, :] = row[:, c * NZ : (c + 1) * NZ]


def first_kernel(right, table, robin_table, robin_index, own, y2, y1, x1, x2, u, out, kap, fx2, fx1, fy1, fy2, sums):
    even_x, even_y, inside = place()
    from_west, from_east = sided(even_x, x1[...], x2[...])
    from_south, from_north = sided(even_y, y1[...], y2[...])
    keys = jnp.concatenate([own[...], from_west, from_east, from_south, from_north], 0)
    pick = (iota((NZ, NZ), 0) == iota((NZ, NZ), 1) // BLOCK).astype(F32)
    keys = jnp.dot(keys, pick, precision=EXACT, preferred_element_type=F32)
    found = jnp.zeros_like(keys)
    for m in range(MATERIALS):
        found = jnp.where(jnp.abs(keys - m) < 0.5, table[m], found)
    kap[...] = jnp.zeros_like(kap)
    kap[0:4, :] = found[0:4]
    for b in range(2):
        own_of = lambda a, c: found[2 * a + c : 2 * a + c + 1]
        kap[4 + b : 5 + b, :] = jnp.where(inside[0] > 0, found[10 + b : 11 + b], own_of(0, b))
        kap[6 + b : 7 + b, :] = jnp.where(inside[1] > 0, found[16 + b : 17 + b], own_of(1, b))
        kap[8 + b : 9 + b, :] = jnp.where(inside[2] > 0, found[25 + 2 * b : 26 + 2 * b], own_of(b, 0))
        kap[10 + b : 11 + b, :] = jnp.where(inside[3] > 0, found[32 + 2 * b : 33 + 2 * b], own_of(b, 1))
    coef = Coefficients(kap)
    relax(coef, inside, robin_of(robin_index, robin_table), u, right, True)
    contribute(coef, inside, u, right, sums, out)
    faces(even_x, even_y, u, (fx2, fx1, fy1, fy2))


def faces(even_x, even_y, u, sends):
    sx2, sx1, sy1, sy2 = sends
    for i in range(CX):
        south, north = u[i][:1], u[i][CY - 1 :]
        sy1[i : i + 1, :] = jnp.where(even_y, north, south)
        sy2[i : i + 1, :] = jnp.where(even_y, south, north)
    sx1[0:CY, :] = jnp.where(even_x, u[CX - 1], u[0])
    sx2[0:CY, :] = jnp.where(even_x, u[0], u[CX - 1])


def join_kernel(x1, x2, out):
    out[0:8, :] = x1[...]
    out[8:16, :] = x2[...]


def ride_kernel(x2, x1, y1, y2, far, fx2, fx1, fy1, fy2, px2, px1, py1, py2):
    even_x, even_y, _ = place()
    east = sided(even_x, x1[...], x2[...])[1][4:8]
    north = sided(even_y, y1[...], y2[...])[1][4:8]
    corner = sided(even_x, far[0:8], far[8:16])[1][4:8]
    for out, face in ((px2, fx2), (px1, fx1)):
        out[0:CY, :] = face[...]
        out[CY : CY + 4, :] = east
        out[CY + 4 : CY + 8, :] = corner
    for out, face in ((py1, fy1), (py2, fy2)):
        out[0:CX, :] = face[...]
        out[CX : CX + 4, :] = north
        out[CX + 4 : CX + 8, :] = corner
        out[CX + 8 : CX + 12, :] = east
        out[CX + 12 : CX + 16, :] = jnp.zeros((4, NZ), F32)


def widen(even_x, even_y, pays, far, seen, rows, shifted):
    own, x2, x1, y1, y2 = pays
    count = rows.shape[1]
    narrow_count = lax.axis_size("narrow")
    wide_count = count // narrow_count
    west, east = (p[4:8] for p in sided(even_x, x1[...], x2[...]))
    south, north = (p[4:8] for p in sided(even_y, y1[...], y2[...]))
    corners = [p[4:8] for p in sided(even_x, far[0:8], far[8:16])]
    beyond_x = sided(even_x, seen[1][...], seen[0][...])[1]
    below, above = sided(even_y, seen[2][...], seen[3][...])
    held = (
        own[4:8], east, north, corners[1],
        west, corners[0],
        beyond_x[CY : CY + 4], beyond_x[CY + 4 : CY + 8],
        south, below[CX + 8 : CX + 12],
        above[CX : CX + 4], above[CX + 4 : CX + 8],
    )
    rows[...] = jnp.zeros_like(rows)
    for k, piece in enumerate(held):
        for c in range(count // NZ):
            rows[k : k + 1, c * NZ : (c + 1) * NZ] = piece[c : c + 1]
    at = iota((16, count), 1)
    at_x, at_y = at // narrow_count, at % narrow_count
    value = rows[...]
    for t, (i, j) in enumerate(SHIFTS):
        x, y = at_x + (i - 1), at_y + (j - 1)
        fits = (x >= 0) & (x < wide_count) & (y >= 0) & (y < narrow_count)
        moved = rolled(value, -((i - 1) * narrow_count + j - 1), 1)
        shifted[16 * t : 16 * t + 16, :] = jnp.where(fits, moved, 0.0)


def window(every, shifted):
    product = jnp.dot(shifted[...], every[...], precision=EXACT, preferred_element_type=F32)
    lane = iota((16, NZ), 1)
    picked = jnp.zeros((16, NZ), F32)
    for t, (i, j) in enumerate(SHIFTS):
        picked = picked + jnp.where(lane == 4 * i + j, product[16 * t : 16 * t + 16], 0.0)
    value = jnp.sum(picked, axis=1, keepdims=True)
    return [jnp.broadcast_to(value[k : k + 1], (CY, NZ)) for k in range(12)]


def correct(even_x, even_y, value, old, new, seen):
    low, high = eta_pair()
    v00, v10, v01, v11, w0, w1, e0, e1, s0, s1, n0, n1 = value
    ramp = lambda first, second: first * low + second * high
    west, east, south, north = ramp(v00, v01), ramp(v10, v11), ramp(v00, v10), ramp(v01, v11)
    for i in range(CX):
        new[i] = old[i] + ((1.0 - row_at(i)) * west + row_at(i) * east)
    seen_x = sided(even_x, seen[1][0:CY], seen[0][0:CY])
    seen_y = sided(even_y, seen[2][0:CX], seen[3][0:CX])
    return (
        seen_x[0] + (NEAR * ramp(w0, w1) + FAR * west),
        seen_x[1] + (FAR * east + NEAR * ramp(e0, e1)),
        seen_y[0] + (NEAR * ramp(s0, s1) + FAR * south),
        seen_y[1] + (FAR * north + NEAR * ramp(n0, n1)),
    )


def second_kernel(
    right, robin_table, robin_index, kap, old, every, own, x2, x1, y1, y2, far, q2, q1, r1, r2,
    u, out, shifted, fx2, fx1, fy1, fy2, rows, source, sums,
):
    even_x, even_y, inside = place()
    seen = (q2, q1, r1, r2)
    widen(even_x, even_y, (own, x2, x1, y1, y2), far, seen, rows, shifted)
    value = window(every, shifted)
    west, east, south, north = correct(even_x, even_y, value, old, u, seen)
    robin = robin_of(robin_index, robin_table)
    coef = Coefficients(kap)
    for i in range(CX):
        a, here = i // BLOCK, u[i]
        total = right[i]
        trace = inside[2] * (coef.south[a] * south[i : i + 1] + robin[1] * here)
        total = total + jnp.where(coef.at_y == 0, trace, 0.0)
        trace = inside[3] * (coef.north[a] * north[i : i + 1] + robin[1] * here)
        total = total + jnp.where(coef.at_y == CY - 1, trace, 0.0)
        if i == 0:
            total = total + inside[0] * (coef.x[0] * west + robin[0] * here)
        if i == CX - 1:
            total = total + inside[1] * (coef.x[CX] * east + robin[0] * here)
        source[i] = total
    relax(coef, inside, robin, u, source, False)
    contribute(coef, inside, u, right, sums, out)
    faces(even_x, even_y, u, (fx2, fx1, fy1, fy2))


def last_kernel(right, kap, old, every, shifted, q2, q1, r1, r2, answer, out, u):
    even_x, even_y, inside = place()
    value = window(every, shifted)
    west, east, south, north = correct(even_x, even_y, value, old, u, (q2, q1, r1, r2))
    coef = Coefficients(kap)
    for i in range(CX):
        a = i // BLOCK
        left = right[i] - coef.total(i) * u[i] + coef.coupling(u, i)
        left = left + jnp.where(coef.at_y == 0, inside[2] * coef.south[a] * south[i : i + 1], 0.0)
        left = left + jnp.where(coef.at_y == CY - 1, inside[3] * coef.north[a] * north[i : i + 1], 0.0)
        if i == 0:
            left = left + inside[0] * coef.x[0] * west
        if i == CX - 1:
            left = left + inside[1] * coef.x[CX] * east
        out[i] = left.astype(jnp.bfloat16)
        answer[i] = u[i].astype(jnp.bfloat16)


def call(kernel, out_shape, spaces, scratch=()):
    return pl.pallas_call(
        kernel,
        out_shape=out_shape,
        in_specs=list(spaces),
        out_specs=jax.tree.map(lambda _: VMEM, out_shape),
        scratch_shapes=list(scratch),
        interpret=INTERPRET,
        compiler_params=pltpu.CompilerParams(vmem_limit_bytes=GRANT),
    )


def swap_pairs(peers, start):
    pairs = []
    for i in range(start, peers - 1, 2):
        pairs += [(i, i + 1), (i + 1, i)]
    return pairs


def swaps(sx2, sx1, sy1, sy2):
    wide_count, narrow_count = lax.axis_size("wide"), lax.axis_size("narrow")
    x2 = lax.ppermute(sx2, "wide", swap_pairs(wide_count, 1))
    x1 = lax.ppermute(sx1, "wide", swap_pairs(wide_count, 0))
    y1 = lax.ppermute(sy1, "narrow", swap_pairs(narrow_count, 0))
    y2 = lax.ppermute(sy2, "narrow", swap_pairs(narrow_count, 1))
    return x2, x1, y1, y2


def everywhere(values):
    return lax.all_to_all(values, ("wide", "narrow"), 0, 0, tiled=True)


def body(right_side, labels, material_table, robin_table, robin_index, coarse_rows):
    count = coarse_rows.shape[1]
    narrow_count = lax.axis_size("narrow")
    shape = lambda *dims: jax.ShapeDtypeStruct(dims, F32)
    scratch = lambda *dims: pltpu.VMEM(dims, F32)
    field, face, gathered = shape(CX, CY, NZ), shape(CY, NZ), shape(count, NZ)
    index = robin_index[0, 0]
    pay = call(pack_kernel, shape(8, NZ), [VMEM] * 2)(labels, coarse_rows)
    x2, x1, y1, y2 = swaps(pay, pay, pay, pay)
    both = call(join_kernel, shape(16, NZ), [VMEM] * 2)(x1, x2)
    far = lax.ppermute(both, "narrow", [(i + 1, i) for i in range(narrow_count - 1)])
    u, sent, kap, *edges = call(
        first_kernel,
        (field, gathered, shape(16, NZ), face, face, face, face),
        [VMEM] + [SMEM] * 3 + [VMEM] * 5,
        [scratch(16, NZ)],
    )(right_side, material_table, robin_table, index, pay, y2, y1, x1, x2)
    every = everywhere(sent)
    edges = call(
        ride_kernel, (shape(CY + 8, NZ),) * 2 + (shape(CX + 16, NZ),) * 2, [VMEM] * 9
    )(x2, x1, y1, y2, far, *edges)
    seen = swaps(*edges)
    u, sent, shifted, *edges = call(
        second_kernel,
        (field, gathered, shape(16 * len(SHIFTS), count), face, face, face, face),
        [VMEM] + [SMEM] * 2 + [VMEM] * 13,
        [scratch(16, count), scratch(CX, CY, NZ), scratch(16, NZ)],
    )(right_side, robin_table, index, kap, u, every, pay, x2, x1, y1, y2, far, *seen)
    every = everywhere(sent)
    seen = swaps(*edges)
    half = jax.ShapeDtypeStruct((CX, CY, NZ), jnp.bfloat16)
    return call(last_kernel, (half, half), [VMEM] * 9, [scratch(CX, CY, NZ)])(
        right_side, kap, u, every, shifted, *seen
    )


def solution(mesh):
    placed = (
        P("wide", "narrow", None),
        P("wide", "narrow", None),
        P(),
        P(),
        P("wide", "narrow", None),
        P(("wide", "narrow"), None),
    )
    return jax.shard_map(
        body,
        mesh=mesh,
        in_specs=placed,
        out_specs=(P("wide", "narrow", None), P("wide", "narrow", None)),
        check_vma=False,
    )
```

```python
import jax
import jax.numpy as jnp
from jax import lax
from jax.experimental import pallas as pl
from jax.experimental.pallas import tpu as pltpu
from jax.sharding import PartitionSpec as P


BLOCK = 8
SWEEPS = 4
CX = 16
CY = 16
NZ = 128
MATERIALS = 16
NEAR = 0.5 / 16
FAR = 15.5 / 16
INTERPRET = False
GRANT = 8 * 1024 * 1024
EXACT = lax.Precision.HIGHEST
F32 = jnp.float32
SHIFTS = [(i, j) for i in range(4) for j in range(4) if i in (1, 2) or j in (1, 2)]

VMEM = pl.BlockSpec(memory_space=pltpu.VMEM)
SMEM = pl.BlockSpec(memory_space=pltpu.SMEM)


def row_at(i):
    return (i + 0.5) / CX


def iota(shape, axis):
    return lax.broadcasted_iota(jnp.int32, shape, axis)


def rolled(value, shift, axis):
    return pltpu.roll(value, shift % value.shape[axis], axis)


def place():
    wide, narrow = lax.axis_index("wide"), lax.axis_index("narrow")
    last_wide, last_narrow = lax.axis_size("wide") - 1, lax.axis_size("narrow") - 1
    inside = tuple(
        jnp.where(flag, F32(1.0), F32(0.0))
        for flag in (wide > 0, wide < last_wide, narrow > 0, narrow < last_narrow)
    )
    return wide % 2 == 0, narrow % 2 == 0, inside


def sided(even, first, second):
    return jnp.where(even, second, first), jnp.where(even, first, second)


def eta_pair():
    eta = (iota((CY, NZ), 0).astype(F32) + 0.5) / CY
    return 1.0 - eta, eta


def robin_of(robin_index, robin_table):
    return robin_table[robin_index[0]], robin_table[robin_index[1]]


class Coefficients:
    def __init__(self, kap):
        row = lambda r: jnp.broadcast_to(kap[r : r + 1, :], (BLOCK, NZ))
        tile = lambda low, high: jnp.concatenate([row(low), row(high)], 0)
        at_y, at_z = iota((CY, NZ), 0), iota((CY, NZ), 1)
        both = (tile(0, 1), tile(2, 3))
        self.x = (
            [0.5 * (both[0] + tile(4, 5))]
            + [both[0]] * 7
            + [0.5 * (both[0] + both[1])]
            + [both[1]] * 7
            + [0.5 * (both[1] + tile(6, 7))]
        )
        self.south, self.north, self.below, self.above = [], [], [], []
        self.rest = []
        for a in range(2):
            k = both[a]
            flipped = tile(2 * a + 1, 2 * a)
            middle = 0.5 * (k + flipped)
            south = jnp.where(at_y == 0, 0.5 * (k + tile(8 + a, 8 + a)), jnp.where(at_y == BLOCK, middle, k))
            north = jnp.where(
                at_y == CY - 1, 0.5 * (k + tile(10 + a, 10 + a)), jnp.where(at_y == BLOCK - 1, middle, k)
            )
            below = jnp.where(at_z == 0, k, 0.5 * (k + rolled(k, 1, 1)))
            above = jnp.where(at_z == NZ - 1, k, 0.5 * (k + rolled(k, -1, 1)))
            self.south.append(south)
            self.north.append(north)
            self.rest.append(south + north + below + above)
            self.below.append(jnp.where(at_z == 0, 0.0, below))
            self.above.append(jnp.where(at_z == NZ - 1, 0.0, above))
        self.south_in = [jnp.where(at_y == 0, 0.0, c) for c in self.south]
        self.north_in = [jnp.where(at_y == CY - 1, 0.0, c) for c in self.north]
        self.at_y = at_y
        self.totals = {}

    def total(self, i):
        key = i if i in (0, 7, 8, 15) else i // BLOCK + 20
        if key not in self.totals:
            self.totals[key] = 1.0 + self.x[i] + self.x[i + 1] + self.rest[i // BLOCK]
        return self.totals[key]

    def coupling(self, u, i):
        a, here = i // BLOCK, u[i]
        total = self.south_in[a] * rolled(here, 1, 0) + self.north_in[a] * rolled(here, -1, 0)
        total = total + self.below[a] * rolled(here, 1, 1) + self.above[a] * rolled(here, -1, 1)
        if i > 0:
            total = total + self.x[i] * u[i - 1]
        if i < CX - 1:
            total = total + self.x[i + 1] * u[i + 1]
        return total


def relax(coef, inside, robin, u, source, first):
    at_y = coef.at_y
    side_y = robin[1] * (
        jnp.where(at_y == 0, inside[2], 0.0) + jnp.where(at_y == CY - 1, inside[3], 0.0)
    )
    inverse = {}
    for i in range(CX):
        key = i if i in (0, 7, 8, 15) else i // BLOCK + 20
        if key not in inverse:
            diagonal = coef.total(i) + side_y
            if i == 0:
                diagonal = diagonal + robin[0] * inside[0]
            if i == CX - 1:
                diagonal = diagonal + robin[0] * inside[1]
            inverse[key] = 1.0 / diagonal
        inverse[i + 100] = inverse[key]
    odd = (iota((CY, NZ), 0) + iota((CY, NZ), 1)) % 2
    masks = (odd == 0, odd == 1)
    for half in range(2 * SWEEPS):
        for i in range(CX):
            mask = masks[(i + half) % 2]
            if first and half == 0:
                u[i] = jnp.where(mask, source[i] * inverse[i + 100], 0.0)
            else:
                update = (source[i] + coef.coupling(u, i)) * inverse[i + 100]
                u[i] = jnp.where(mask, update, u[i])


def contribute(coef, inside, u, right, sums, out):
    weights = eta_pair()
    zero = jnp.zeros((CY, NZ), F32)
    own, south, north = [zero, zero], [zero, zero], [zero, zero]
    for i in range(CX):
        a, here = i // BLOCK, u[i]
        left = right[i] - coef.total(i) * here + coef.coupling(u, i)
        low, high = coef.south[a] * here, coef.north[a] * here
        for side, weight in enumerate((1.0 - row_at(i), row_at(i))):
            own[side] = own[side] + weight * left
            south[side] = south[side] + weight * low
            north[side] = north[side] + weight * high
    across = lambda value, b: jnp.sum(value * weights[b], axis=0, keepdims=True)
    west, east = inside[0] * coef.x[0] * u[0], inside[1] * coef.x[CX] * u[CX - 1]
    west_row = [across(west, b) for b in range(2)]
    east_row = [across(east, b) for b in range(2)]
    south_row = [inside[2] * south[a][:1] for a in range(2)]
    north_row = [inside[3] * north[a][CY - 1 :] for a in range(2)]
    sums[...] = jnp.zeros_like(sums)
    for a in range(2):
        for b in range(2):
            near_x, near_y = (west_row, east_row)[a][b], (south_row, north_row)[b][a]
            at = (1 + a) * 4 + 1 + b
            sums[at : at + 1, :] = across(own[a], b) + FAR * (near_x + near_y)
    for b in range(2):
        sums[1 + b : 2 + b, :] = NEAR * west_row[b]
        sums[13 + b : 14 + b, :] = NEAR * east_row[b]
    for a in range(2):
        at = (1 + a) * 4
        sums[at : at + 1, :] = NEAR * south_row[a]
        sums[at + 3 : at + 4, :] = NEAR * north_row[a]
    column = jnp.sum(sums[...], axis=1, keepdims=True)
    spread = jnp.where(iota((16, NZ), 0) == iota((16, NZ), 1), column, 0.0)
    out[...] = jnp.broadcast_to(jnp.sum(spread, axis=0, keepdims=True), out.shape)


def pack_kernel(labels, row, pay):
    pay[...] = jnp.zeros_like(pay)
    for a in range(2):
        pay[2 * a : 2 * a + 2, 0 : labels.shape[2]] = labels[a].astype(F32)
    for c in range(row.shape[1] // NZ):
        pay[4 + c : 5 + c, :] = row[:, c * NZ : (c + 1) * NZ]


def first_kernel(
    right, table, robin_table, robin_index, own, y2, y1, x1, x2,
    u, out, kap, fx2, fx1, fy1, fy2, sums,
):
    even_x, even_y, inside = place()
    from_west, from_east = sided(even_x, x1[...], x2[...])
    from_south, from_north = sided(even_y, y1[...], y2[...])
    keys = jnp.concatenate([own[...], from_west, from_east, from_south, from_north], 0)
    pick = (iota((NZ, NZ), 0) == iota((NZ, NZ), 1) // BLOCK).astype(F32)
    keys = jnp.dot(keys, pick, precision=EXACT, preferred_element_type=F32)
    found = jnp.zeros_like(keys)
    for m in range(MATERIALS):
        found = jnp.where(jnp.abs(keys - m) < 0.5, table[m], found)
    kap[...] = jnp.zeros_like(kap)
    kap[0:4, :] = found[0:4]
    for b in range(2):
        own_of = lambda a, c: found[2 * a + c : 2 * a + c + 1]
        kap[4 + b : 5 + b, :] = jnp.where(inside[0] > 0, found[10 + b : 11 + b], own_of(0, b))
        kap[6 + b : 7 + b, :] = jnp.where(inside[1] > 0, found[16 + b : 17 + b], own_of(1, b))
        kap[8 + b : 9 + b, :] = jnp.where(inside[2] > 0, found[25 + 2 * b : 26 + 2 * b], own_of(b, 0))
        kap[10 + b : 11 + b, :] = jnp.where(inside[3] > 0, found[32 + 2 * b : 33 + 2 * b], own_of(b, 1))
    coef = Coefficients(kap)
    relax(coef, inside, robin_of(robin_index, robin_table), u, right, True)
    contribute(coef, inside, u, right, sums, out)
    faces(even_x, even_y, u, (fx2, fx1, fy1, fy2))


def faces(even_x, even_y, u, sends):
    sx2, sx1, sy1, sy2 = sends
    for i in range(CX):
        south, north = u[i][:1], u[i][CY - 1 :]
        sy1[i : i + 1, :] = jnp.where(even_y, north, south)
        sy2[i : i + 1, :] = jnp.where(even_y, south, north)
    sx1[0:CY, :] = jnp.where(even_x, u[CX - 1], u[0])
    sx2[0:CY, :] = jnp.where(even_x, u[0], u[CX - 1])


def ride_y_kernel(x2, x1, y1, y2, fy1, fy2, py1, py2):
    even_x, even_y, _ = place()
    west, east = (p[4:8] for p in sided(even_x, x1[...], x2[...]))
    north = sided(even_y, y1[...], y2[...])[1][4:8]
    for out, face in ((py1, fy1), (py2, fy2)):
        out[0:CX, :] = face[...]
        for k, piece in enumerate((north, east, west, jnp.zeros((4, NZ), F32))):
            out[CX + 4 * k : CX + 4 * k + 4, :] = piece


def ride_x_kernel(x2, x1, r1, r2, fx2, fx1, px2, px1):
    even_x, even_y, _ = place()
    east = sided(even_x, x1[...], x2[...])[1][4:8]
    above = sided(even_y, r1[...], r2[...])[1]
    for out, face in ((px2, fx2), (px1, fx1)):
        out[0:CY, :] = face[...]
        pieces = (east, above[CX + 4 : CX + 8], above[CX : CX + 4], jnp.zeros((4, NZ), F32))
        for k, piece in enumerate(pieces):
            out[CY + 4 * k : CY + 4 * k + 4, :] = piece


def widen_kernel(own, x2, x1, y1, y2, q2, q1, r1, r2, shifted, rows):
    even_x, even_y, _ = place()
    count = rows.shape[1]
    narrow_count = lax.axis_size("narrow")
    wide_count = count // narrow_count
    west, east = (p[4:8] for p in sided(even_x, x1[...], x2[...]))
    south, north = (p[4:8] for p in sided(even_y, y1[...], y2[...]))
    beyond = sided(even_x, q1[...], q2[...])[1]
    below, above = sided(even_y, r1[...], r2[...])
    taken = lambda value, k: value[CX + 4 * k : CX + 4 * k + 4]
    held = (
        own[4:8], east, north, taken(above, 1),
        west, taken(above, 2),
        taken(beyond, 0), taken(beyond, 1),
        south, taken(below, 1),
        taken(above, 0), taken(beyond, 2),
    )
    rows[...] = jnp.zeros_like(rows)
    for k, piece in enumerate(held):
        for c in range(count // NZ):
            rows[k : k + 1, c * NZ : (c + 1) * NZ] = piece[c : c + 1]
    at = iota((16, count), 1)
    at_x, at_y = at // narrow_count, at % narrow_count
    value = rows[...]
    for t, (i, j) in enumerate(SHIFTS):
        x, y = at_x + (i - 1), at_y + (j - 1)
        fits = (x >= 0) & (x < wide_count) & (y >= 0) & (y < narrow_count)
        moved = rolled(value, -((i - 1) * narrow_count + j - 1), 1)
        shifted[16 * t : 16 * t + 16, :] = jnp.where(fits, moved, 0.0)


def window(every, shifted):
    product = jnp.dot(shifted[...], every[...], precision=EXACT, preferred_element_type=F32)
    lane = iota((16, NZ), 1)
    picked = jnp.zeros((16, NZ), F32)
    for t, (i, j) in enumerate(SHIFTS):
        picked = picked + jnp.where(lane == 4 * i + j, product[16 * t : 16 * t + 16], 0.0)
    value = jnp.sum(picked, axis=1, keepdims=True)
    return [jnp.broadcast_to(value[k : k + 1], (CY, NZ)) for k in range(12)]


def correct(even_x, even_y, value, old, new, seen):
    low, high = eta_pair()
    v00, v10, v01, v11, w0, w1, e0, e1, s0, s1, n0, n1 = value
    ramp = lambda first, second: first * low + second * high
    west, east, south, north = ramp(v00, v01), ramp(v10, v11), ramp(v00, v10), ramp(v01, v11)
    for i in range(CX):
        new[i] = old[i] + ((1.0 - row_at(i)) * west + row_at(i) * east)
    seen_x = sided(even_x, seen[1][0:CY], seen[0][0:CY])
    seen_y = sided(even_y, seen[2][0:CX], seen[3][0:CX])
    return (
        seen_x[0] + (NEAR * ramp(w0, w1) + FAR * west),
        seen_x[1] + (FAR * east + NEAR * ramp(e0, e1)),
        seen_y[0] + (NEAR * ramp(s0, s1) + FAR * south),
        seen_y[1] + (FAR * north + NEAR * ramp(n0, n1)),
    )


def second_kernel(
    right, robin_table, robin_index, kap, old, every, shifted, q2, q1, r1, r2,
    u, out, fx2, fx1, fy1, fy2, source, sums,
):
    even_x, even_y, inside = place()
    seen = (q2, q1, r1, r2)
    value = window(every, shifted)
    west, east, south, north = correct(even_x, even_y, value, old, u, seen)
    robin = robin_of(robin_index, robin_table)
    coef = Coefficients(kap)
    for i in range(CX):
        a, here = i // BLOCK, u[i]
        total = right[i]
        trace = inside[2] * (coef.south[a] * south[i : i + 1] + robin[1] * here)
        total = total + jnp.where(coef.at_y == 0, trace, 0.0)
        trace = inside[3] * (coef.north[a] * north[i : i + 1] + robin[1] * here)
        total = total + jnp.where(coef.at_y == CY - 1, trace, 0.0)
        if i == 0:
            total = total + inside[0] * (coef.x[0] * west + robin[0] * here)
        if i == CX - 1:
            total = total + inside[1] * (coef.x[CX] * east + robin[0] * here)
        source[i] = total
    relax(coef, inside, robin, u, source, False)
    contribute(coef, inside, u, right, sums, out)
    faces(even_x, even_y, u, (fx2, fx1, fy1, fy2))


def last_kernel(right, kap, old, every, shifted, q2, q1, r1, r2, answer, out, u):
    even_x, even_y, inside = place()
    value = window(every, shifted)
    west, east, south, north = correct(even_x, even_y, value, old, u, (q2, q1, r1, r2))
    coef = Coefficients(kap)
    for i in range(CX):
        a = i // BLOCK
        left = right[i] - coef.total(i) * u[i] + coef.coupling(u, i)
        left = left + jnp.where(coef.at_y == 0, inside[2] * coef.south[a] * south[i : i + 1], 0.0)
        left = left + jnp.where(coef.at_y == CY - 1, inside[3] * coef.north[a] * north[i : i + 1], 0.0)
        if i == 0:
            left = left + inside[0] * coef.x[0] * west
        if i == CX - 1:
            left = left + inside[1] * coef.x[CX] * east
        out[i] = left.astype(jnp.bfloat16)
        answer[i] = u[i].astype(jnp.bfloat16)


def call(kernel, out_shape, spaces, scratch=()):
    return pl.pallas_call(
        kernel,
        out_shape=out_shape,
        in_specs=list(spaces),
        out_specs=jax.tree.map(lambda _: VMEM, out_shape),
        scratch_shapes=list(scratch),
        interpret=INTERPRET,
        compiler_params=pltpu.CompilerParams(vmem_limit_bytes=GRANT),
    )


def swap_pairs(peers, start):
    pairs = []
    for i in range(start, peers - 1, 2):
        pairs += [(i, i + 1), (i + 1, i)]
    return pairs


def swap(array, axis, start):
    return lax.ppermute(array, axis, swap_pairs(lax.axis_size(axis), start))


def swaps(sx2, sx1, sy1, sy2):
    x2 = swap(sx2, "wide", 1)
    x1 = swap(sx1, "wide", 0)
    y1 = swap(sy1, "narrow", 0)
    y2 = swap(sy2, "narrow", 1)
    return x2, x1, y1, y2


def everywhere(values):
    return lax.all_to_all(values, ("wide", "narrow"), 0, 0, tiled=True)


def body(right_side, labels, material_table, robin_table, robin_index, coarse_rows):
    count = coarse_rows.shape[1]
    shape = lambda *dims: jax.ShapeDtypeStruct(dims, F32)
    scratch = lambda *dims: pltpu.VMEM(dims, F32)
    field, face, gathered = shape(CX, CY, NZ), shape(CY, NZ), shape(count, NZ)
    index = robin_index[0, 0]
    pay = call(pack_kernel, shape(8, NZ), [VMEM] * 2)(labels, coarse_rows)
    x2, x1, y1, y2 = swaps(pay, pay, pay, pay)
    u, sent, kap, fx2, fx1, fy1, fy2 = call(
        first_kernel,
        (field, gathered, shape(16, NZ), face, face, face, face),
        [VMEM] + [SMEM] * 3 + [VMEM] * 5,
        [scratch(16, NZ)],
    )(right_side, material_table, robin_table, index, pay, y2, y1, x1, x2)
    every = everywhere(sent)
    ridden = (shape(CY + 16, NZ),) * 2
    py1, py2 = call(ride_y_kernel, ridden, [VMEM] * 6)(x2, x1, y1, y2, fy1, fy2)
    r1 = swap(py1, "narrow", 0)
    r2 = swap(py2, "narrow", 1)
    px2, px1 = call(ride_x_kernel, ridden, [VMEM] * 6)(x2, x1, r1, r2, fx2, fx1)
    seen = (swap(px2, "wide", 1), swap(px1, "wide", 0), r1, r2)
    shifted = call(
        widen_kernel, shape(16 * len(SHIFTS), count), [VMEM] * 9, [scratch(16, count)]
    )(pay, x2, x1, y1, y2, *seen)
    u, sent, *edges = call(
        second_kernel,
        (field, gathered, face, face, face, face),
        [VMEM] + [SMEM] * 2 + [VMEM] * 8,
        [scratch(CX, CY, NZ), scratch(16, NZ)],
    )(right_side, robin_table, index, kap, u, every, shifted, *seen)
    every = everywhere(sent)
    seen = swaps(*edges)
    half = jax.ShapeDtypeStruct((CX, CY, NZ), jnp.bfloat16)
    return call(last_kernel, (half, half), [VMEM] * 9, [scratch(CX, CY, NZ)])(
        right_side, kap, u, every, shifted, *seen
    )


def solution(mesh):
    placed = (
        P("wide", "narrow", None),
        P("wide", "narrow", None),
        P(),
        P(),
        P("wide", "narrow", None),
        P(("wide", "narrow"), None),
    )
    return jax.shard_map(
        body,
        mesh=mesh,
        in_specs=placed,
        out_specs=(P("wide", "narrow", None), P("wide", "narrow", None)),
        check_vma=False,
    )
```

```python
import jax
import jax.numpy as jnp
from jax import lax
from jax.experimental import pallas as pl
from jax.experimental.pallas import tpu as pltpu
from jax.sharding import Mesh
from jax.sharding import PartitionSpec as P


BLOCK = 8
SWEEPS = 4
CX = 16
CY = 16
NZ = 128
MATERIALS = 16
NEAR = 0.5 / 16
FAR = 15.5 / 16
INTERPRET = False
GRANT = 8 * 1024 * 1024
EXACT = lax.Precision.HIGHEST
F32 = jnp.float32
WIDE = ("half", "plane")
SHIFTS = [(i, j) for i in range(4) for j in range(4) if i in (1, 2) or j in (1, 2)]

VMEM = pl.BlockSpec(memory_space=pltpu.VMEM)
SMEM = pl.BlockSpec(memory_space=pltpu.SMEM)


def row_at(i):
    return (i + 0.5) / CX


def iota(shape, axis):
    return lax.broadcasted_iota(jnp.int32, shape, axis)


def rolled(value, shift, axis):
    return pltpu.roll(value, shift % value.shape[axis], axis)


def place():
    planes, narrow = lax.axis_size("plane"), lax.axis_index("narrow")
    wide = lax.axis_index("half") * planes + lax.axis_index("plane")
    last_wide, last_narrow = lax.axis_size("half") * planes - 1, lax.axis_size("narrow") - 1
    inside = tuple(
        jnp.where(flag, F32(1.0), F32(0.0))
        for flag in (wide > 0, wide < last_wide, narrow > 0, narrow < last_narrow)
    )
    return wide % 2 == 0, narrow % 2 == 0, inside


def sided(even, first, second):
    return jnp.where(even, second, first), jnp.where(even, first, second)


def eta_pair():
    eta = (iota((CY, NZ), 0).astype(F32) + 0.5) / CY
    return 1.0 - eta, eta


def robin_of(robin_index, robin_table):
    return robin_table[robin_index[0]], robin_table[robin_index[1]]


class Coefficients:
    def __init__(self, kap):
        row = lambda r: jnp.broadcast_to(kap[r : r + 1, :], (BLOCK, NZ))
        tile = lambda low, high: jnp.concatenate([row(low), row(high)], 0)
        at_y, at_z = iota((CY, NZ), 0), iota((CY, NZ), 1)
        both = (tile(0, 1), tile(2, 3))
        self.x = (
            [0.5 * (both[0] + tile(4, 5))]
            + [both[0]] * 7
            + [0.5 * (both[0] + both[1])]
            + [both[1]] * 7
            + [0.5 * (both[1] + tile(6, 7))]
        )
        self.south, self.north, self.below, self.above = [], [], [], []
        self.rest = []
        for a in range(2):
            k = both[a]
            flipped = tile(2 * a + 1, 2 * a)
            middle = 0.5 * (k + flipped)
            south = jnp.where(at_y == 0, 0.5 * (k + tile(8 + a, 8 + a)), jnp.where(at_y == BLOCK, middle, k))
            north = jnp.where(
                at_y == CY - 1, 0.5 * (k + tile(10 + a, 10 + a)), jnp.where(at_y == BLOCK - 1, middle, k)
            )
            below = jnp.where(at_z == 0, k, 0.5 * (k + rolled(k, 1, 1)))
            above = jnp.where(at_z == NZ - 1, k, 0.5 * (k + rolled(k, -1, 1)))
            self.south.append(south)
            self.north.append(north)
            self.rest.append(south + north + below + above)
            self.below.append(jnp.where(at_z == 0, 0.0, below))
            self.above.append(jnp.where(at_z == NZ - 1, 0.0, above))
        self.south_in = [jnp.where(at_y == 0, 0.0, c) for c in self.south]
        self.north_in = [jnp.where(at_y == CY - 1, 0.0, c) for c in self.north]
        self.at_y = at_y
        self.totals = {}

    def total(self, i):
        key = i if i in (0, 7, 8, 15) else i // BLOCK + 20
        if key not in self.totals:
            self.totals[key] = 1.0 + self.x[i] + self.x[i + 1] + self.rest[i // BLOCK]
        return self.totals[key]

    def coupling(self, u, i):
        a, here = i // BLOCK, u[i]
        total = self.south_in[a] * rolled(here, 1, 0) + self.north_in[a] * rolled(here, -1, 0)
        total = total + self.below[a] * rolled(here, 1, 1) + self.above[a] * rolled(here, -1, 1)
        if i > 0:
            total = total + self.x[i] * u[i - 1]
        if i < CX - 1:
            total = total + self.x[i + 1] * u[i + 1]
        return total


def relax(coef, inside, robin, u, source, first):
    at_y = coef.at_y
    side_y = robin[1] * (
        jnp.where(at_y == 0, inside[2], 0.0) + jnp.where(at_y == CY - 1, inside[3], 0.0)
    )
    inverse = {}
    for i in range(CX):
        key = i if i in (0, 7, 8, 15) else i // BLOCK + 20
        if key not in inverse:
            diagonal = coef.total(i) + side_y
            if i == 0:
                diagonal = diagonal + robin[0] * inside[0]
            if i == CX - 1:
                diagonal = diagonal + robin[0] * inside[1]
            inverse[key] = 1.0 / diagonal
        inverse[i + 100] = inverse[key]
    odd = (iota((CY, NZ), 0) + iota((CY, NZ), 1)) % 2
    masks = (odd == 0, odd == 1)
    for half in range(2 * SWEEPS):
        for i in range(CX):
            mask = masks[(i + half) % 2]
            if first and half == 0:
                u[i] = jnp.where(mask, source[i] * inverse[i + 100], 0.0)
            else:
                update = (source[i] + coef.coupling(u, i)) * inverse[i + 100]
                u[i] = jnp.where(mask, update, u[i])


def contribute(coef, inside, u, right, sums, out):
    weights = eta_pair()
    zero = jnp.zeros((CY, NZ), F32)
    own, south, north = [zero, zero], [zero, zero], [zero, zero]
    for i in range(CX):
        a, here = i // BLOCK, u[i]
        left = right[i] - coef.total(i) * here + coef.coupling(u, i)
        low, high = coef.south[a] * here, coef.north[a] * here
        for side, weight in enumerate((1.0 - row_at(i), row_at(i))):
            own[side] = own[side] + weight * left
            south[side] = south[side] + weight * low
            north[side] = north[side] + weight * high
    across = lambda value, b: jnp.sum(value * weights[b], axis=0, keepdims=True)
    west, east = inside[0] * coef.x[0] * u[0], inside[1] * coef.x[CX] * u[CX - 1]
    west_row = [across(west, b) for b in range(2)]
    east_row = [across(east, b) for b in range(2)]
    south_row = [inside[2] * south[a][:1] for a in range(2)]
    north_row = [inside[3] * north[a][CY - 1 :] for a in range(2)]
    sums[...] = jnp.zeros_like(sums)
    for a in range(2):
        for b in range(2):
            near_x, near_y = (west_row, east_row)[a][b], (south_row, north_row)[b][a]
            at = (1 + a) * 4 + 1 + b
            sums[at : at + 1, :] = across(own[a], b) + FAR * (near_x + near_y)
    for b in range(2):
        sums[1 + b : 2 + b, :] = NEAR * west_row[b]
        sums[13 + b : 14 + b, :] = NEAR * east_row[b]
    for a in range(2):
        at = (1 + a) * 4
        sums[at : at + 1, :] = NEAR * south_row[a]
        sums[at + 3 : at + 4, :] = NEAR * north_row[a]
    column = jnp.sum(sums[...], axis=1, keepdims=True)
    spread = jnp.where(iota((16, NZ), 0) == iota((16, NZ), 1) % 16, column, 0.0)
    out[...] = jnp.broadcast_to(jnp.sum(spread, axis=0, keepdims=True), out.shape)


def pack_kernel(labels, row, pay):
    pay[...] = jnp.zeros_like(pay)
    for a in range(2):
        pay[2 * a : 2 * a + 2, 0 : labels.shape[2]] = labels[a].astype(F32)
    for c in range(row.shape[1] // NZ):
        pay[4 + c : 5 + c, :] = row[:, c * NZ : (c + 1) * NZ]


def first_kernel(right, table, robin_table, robin_index, own, y2, y1, x1, x2, u, out, kap, fx2, fx1, fy1, fy2, sums):
    even_x, even_y, inside = place()
    from_west, from_east = sided(even_x, x1[...], x2[...])
    from_south, from_north = sided(even_y, y1[...], y2[...])
    keys = jnp.concatenate([own[...], from_west, from_east, from_south, from_north], 0)
    pick = (iota((NZ, NZ), 0) == iota((NZ, NZ), 1) // BLOCK).astype(F32)
    keys = jnp.dot(keys, pick, precision=EXACT, preferred_element_type=F32)
    found = jnp.zeros_like(keys)
    for m in range(MATERIALS):
        found = jnp.where(jnp.abs(keys - m) < 0.5, table[m], found)
    kap[...] = jnp.zeros_like(kap)
    kap[0:4, :] = found[0:4]
    for b in range(2):
        own_of = lambda a, c: found[2 * a + c : 2 * a + c + 1]
        kap[4 + b : 5 + b, :] = jnp.where(inside[0] > 0, found[10 + b : 11 + b], own_of(0, b))
        kap[6 + b : 7 + b, :] = jnp.where(inside[1] > 0, found[16 + b : 17 + b], own_of(1, b))
        kap[8 + b : 9 + b, :] = jnp.where(inside[2] > 0, found[25 + 2 * b : 26 + 2 * b], own_of(b, 0))
        kap[10 + b : 11 + b, :] = jnp.where(inside[3] > 0, found[32 + 2 * b : 33 + 2 * b], own_of(b, 1))
    coef = Coefficients(kap)
    relax(coef, inside, robin_of(robin_index, robin_table), u, right, True)
    contribute(coef, inside, u, right, sums, out)
    faces(even_x, even_y, u, (fx2, fx1, fy1, fy2))


def faces(even_x, even_y, u, sends):
    sx2, sx1, sy1, sy2 = sends
    for i in range(CX):
        south, north = u[i][:1], u[i][CY - 1 :]
        sy1[i : i + 1, :] = jnp.where(even_y, north, south)
        sy2[i : i + 1, :] = jnp.where(even_y, south, north)
    sx1[0:CY, :] = jnp.where(even_x, u[CX - 1], u[0])
    sx2[0:CY, :] = jnp.where(even_x, u[0], u[CX - 1])


def join_kernel(x1, x2, out):
    out[0:8, :] = x1[...]
    out[8:16, :] = x2[...]


def ride_kernel(x2, x1, y1, y2, far, fx2, fx1, fy1, fy2, px2, px1, py1, py2):
    even_x, even_y, _ = place()
    east = sided(even_x, x1[...], x2[...])[1][4:8]
    north = sided(even_y, y1[...], y2[...])[1][4:8]
    corner = sided(even_x, far[0:8], far[8:16])[1][4:8]
    for out, face in ((px2, fx2), (px1, fx1)):
        out[0:CY, :] = face[...]
        out[CY : CY + 4, :] = east
        out[CY + 4 : CY + 8, :] = corner
    for out, face in ((py1, fy1), (py2, fy2)):
        out[0:CX, :] = face[...]
        out[CX : CX + 4, :] = north
        out[CX + 4 : CX + 8, :] = corner
        out[CX + 8 : CX + 12, :] = east
        out[CX + 12 : CX + 16, :] = jnp.zeros((4, NZ), F32)


def widen_kernel(own, x2, x1, y1, y2, far, q2, q1, r1, r2, shifted, rows, moves):
    even_x, even_y, _ = place()
    seen = (q2, q1, r1, r2)
    count = rows.shape[1]
    narrow_count = lax.axis_size("narrow")
    wide_count = count // narrow_count
    west, east = (p[4:8] for p in sided(even_x, x1[...], x2[...]))
    south, north = (p[4:8] for p in sided(even_y, y1[...], y2[...]))
    corners = [p[4:8] for p in sided(even_x, far[0:8], far[8:16])]
    beyond_x = sided(even_x, seen[1][...], seen[0][...])[1]
    below, above = sided(even_y, seen[2][...], seen[3][...])
    held = (
        own[4:8], east, north, corners[1],
        west, corners[0],
        beyond_x[CY : CY + 4], beyond_x[CY + 4 : CY + 8],
        south, below[CX + 8 : CX + 12],
        above[CX : CX + 4], above[CX + 4 : CX + 8],
    )
    rows[...] = jnp.zeros_like(rows)
    for k, piece in enumerate(held):
        for c in range(count // NZ):
            rows[k : k + 1, c * NZ : (c + 1) * NZ] = piece[c : c + 1]
    at = iota((16, count), 1)
    at_x, at_y = at // narrow_count, at % narrow_count
    value = rows[...]
    for t, (i, j) in enumerate(SHIFTS):
        x, y = at_x + (i - 1), at_y + (j - 1)
        fits = (x >= 0) & (x < wide_count) & (y >= 0) & (y < narrow_count)
        moved = rolled(value, -((i - 1) * narrow_count + j - 1), 1)
        moves[16 * t : 16 * t + 16, :] = jnp.where(fits, moved, 0.0)
    planes = lax.axis_size("plane")
    source, target = iota((count, count), 0), iota((count, count), 1)
    half, plane = target // (narrow_count * planes), target % planes
    wanted = (half * planes + plane) * narrow_count + target // planes % narrow_count
    order = (source == wanted).astype(F32)
    shifted[...] = jnp.dot(moves[...], order, precision=EXACT, preferred_element_type=F32)


def turn_kernel(arrived, out):
    groups = arrived.shape[0] // 8
    mine = iota((8, NZ), 1) // 16 == iota((8, NZ), 0)
    for q in range(groups):
        kept = jnp.where(mine, arrived[8 * q : 8 * q + 8, :], 0.0)
        row = jnp.sum(kept, axis=0, keepdims=True)
        for b in range(out.shape[0] // groups):
            out[b * groups + q : b * groups + q + 1, :] = row


def window(every, shifted, opened):
    mine = iota((8, NZ), 1) // 16 == iota((8, NZ), 0)
    for d in range(every.shape[0]):
        row = jnp.broadcast_to(every[d : d + 1, :], (8, NZ))
        opened[8 * d : 8 * d + 8, :] = jnp.where(mine, row, 0.0)
    product = jnp.dot(shifted[...], opened[...], precision=EXACT, preferred_element_type=F32)
    lane = iota((16, NZ), 1) % 16
    picked = jnp.zeros((16, NZ), F32)
    for t, (i, j) in enumerate(SHIFTS):
        picked = picked + jnp.where(lane == 4 * i + j, product[16 * t : 16 * t + 16], 0.0)
    value = jnp.sum(picked, axis=1, keepdims=True)
    return [jnp.broadcast_to(value[k : k + 1], (CY, NZ)) for k in range(12)]


def correct(even_x, even_y, value, old, new, seen):
    low, high = eta_pair()
    v00, v10, v01, v11, w0, w1, e0, e1, s0, s1, n0, n1 = value
    ramp = lambda first, second: first * low + second * high
    west, east, south, north = ramp(v00, v01), ramp(v10, v11), ramp(v00, v10), ramp(v01, v11)
    for i in range(CX):
        new[i] = old[i] + ((1.0 - row_at(i)) * west + row_at(i) * east)
    seen_x = sided(even_x, seen[1][0:CY], seen[0][0:CY])
    seen_y = sided(even_y, seen[2][0:CX], seen[3][0:CX])
    return (
        seen_x[0] + (NEAR * ramp(w0, w1) + FAR * west),
        seen_x[1] + (FAR * east + NEAR * ramp(e0, e1)),
        seen_y[0] + (NEAR * ramp(s0, s1) + FAR * south),
        seen_y[1] + (FAR * north + NEAR * ramp(n0, n1)),
    )


def second_kernel(
    right, robin_table, robin_index, kap, old, every, shifted, q2, q1, r1, r2,
    u, out, fx2, fx1, fy1, fy2, source, sums, opened,
):
    even_x, even_y, inside = place()
    seen = (q2, q1, r1, r2)
    value = window(every, shifted, opened)
    west, east, south, north = correct(even_x, even_y, value, old, u, seen)
    robin = robin_of(robin_index, robin_table)
    coef = Coefficients(kap)
    for i in range(CX):
        a, here = i // BLOCK, u[i]
        total = right[i]
        trace = inside[2] * (coef.south[a] * south[i : i + 1] + robin[1] * here)
        total = total + jnp.where(coef.at_y == 0, trace, 0.0)
        trace = inside[3] * (coef.north[a] * north[i : i + 1] + robin[1] * here)
        total = total + jnp.where(coef.at_y == CY - 1, trace, 0.0)
        if i == 0:
            total = total + inside[0] * (coef.x[0] * west + robin[0] * here)
        if i == CX - 1:
            total = total + inside[1] * (coef.x[CX] * east + robin[0] * here)
        source[i] = total
    relax(coef, inside, robin, u, source, False)
    contribute(coef, inside, u, right, sums, out)
    faces(even_x, even_y, u, (fx2, fx1, fy1, fy2))


def last_kernel(right, kap, old, every, shifted, q2, q1, r1, r2, answer, out, u, opened):
    even_x, even_y, inside = place()
    value = window(every, shifted, opened)
    west, east, south, north = correct(even_x, even_y, value, old, u, (q2, q1, r1, r2))
    coef = Coefficients(kap)
    for i in range(CX):
        a = i // BLOCK
        left = right[i] - coef.total(i) * u[i] + coef.coupling(u, i)
        left = left + jnp.where(coef.at_y == 0, inside[2] * coef.south[a] * south[i : i + 1], 0.0)
        left = left + jnp.where(coef.at_y == CY - 1, inside[3] * coef.north[a] * north[i : i + 1], 0.0)
        if i == 0:
            left = left + inside[0] * coef.x[0] * west
        if i == CX - 1:
            left = left + inside[1] * coef.x[CX] * east
        out[i] = left.astype(jnp.bfloat16)
        answer[i] = u[i].astype(jnp.bfloat16)


def call(kernel, out_shape, spaces, scratch=()):
    return pl.pallas_call(
        kernel,
        out_shape=out_shape,
        in_specs=list(spaces),
        out_specs=jax.tree.map(lambda _: VMEM, out_shape),
        scratch_shapes=list(scratch),
        interpret=INTERPRET,
        compiler_params=pltpu.CompilerParams(vmem_limit_bytes=GRANT),
    )


def swap_pairs(peers, start):
    pairs = []
    for i in range(start, peers - 1, 2):
        pairs += [(i, i + 1), (i + 1, i)]
    return pairs


def swap(array, axis, start):
    return lax.ppermute(array, axis, swap_pairs(lax.axis_size(axis), start))


def swaps(sx2, sx1, sy1, sy2):
    x2 = swap(sx2, WIDE, 1)
    x1 = swap(sx1, WIDE, 0)
    y1 = swap(sy1, "narrow", 0)
    y2 = swap(sy2, "narrow", 1)
    return x2, x1, y1, y2


def everywhere(values, count):
    near = lax.all_to_all(values, "plane", 0, 0, tiled=True)
    turned = call(turn_kernel, jax.ShapeDtypeStruct((count // 8, NZ), F32), [VMEM])(near)
    return lax.all_to_all(turned, ("half", "narrow"), 0, 0, tiled=True)


def body(right_side, labels, material_table, robin_table, robin_index, coarse_rows):
    count = coarse_rows.shape[1]
    narrow_count = lax.axis_size("narrow")
    shape = lambda *dims: jax.ShapeDtypeStruct(dims, F32)
    scratch = lambda *dims: pltpu.VMEM(dims, F32)
    field, face, mine = shape(CX, CY, NZ), shape(CY, NZ), shape(lax.axis_size("plane"), NZ)
    index = robin_index[0, 0]
    pay = call(pack_kernel, shape(8, NZ), [VMEM] * 2)(labels, coarse_rows)
    x2, x1, y1, y2 = swaps(pay, pay, pay, pay)
    both = call(join_kernel, shape(16, NZ), [VMEM] * 2)(x1, x2)
    far = lax.ppermute(both, "narrow", [(i + 1, i) for i in range(narrow_count - 1)])
    u, sent, kap, *edges = call(
        first_kernel,
        (field, mine, shape(16, NZ), face, face, face, face),
        [VMEM] + [SMEM] * 3 + [VMEM] * 5,
        [scratch(16, NZ)],
    )(right_side, material_table, robin_table, index, pay, y2, y1, x1, x2)
    every = everywhere(sent, count)
    edges = call(
        ride_kernel, (shape(CY + 8, NZ),) * 2 + (shape(CX + 16, NZ),) * 2, [VMEM] * 9
    )(x2, x1, y1, y2, far, *edges)
    seen = swaps(*edges)
    lines = 16 * len(SHIFTS)
    shifted = call(
        widen_kernel, shape(lines, count), [VMEM] * 10, [scratch(16, count), scratch(lines, count)]
    )(pay, x2, x1, y1, y2, far, *seen)
    u, sent, *edges = call(
        second_kernel,
        (field, mine, face, face, face, face),
        [VMEM] + [SMEM] * 2 + [VMEM] * 8,
        [scratch(CX, CY, NZ), scratch(16, NZ), scratch(count, NZ)],
    )(right_side, robin_table, index, kap, u, every, shifted, *seen)
    every = everywhere(sent, count)
    seen = swaps(*edges)
    half = jax.ShapeDtypeStruct((CX, CY, NZ), jnp.bfloat16)
    return call(last_kernel, (half, half), [VMEM] * 9, [scratch(CX, CY, NZ), scratch(count, NZ)])(
        right_side, kap, u, every, shifted, *seen
    )


def solution(mesh):
    devices = mesh.devices
    split = Mesh(devices.reshape(2, devices.shape[0] // 2, -1), (*WIDE, "narrow"))
    placed = (
        P(WIDE, "narrow", None),
        P(WIDE, "narrow", None),
        P(),
        P(),
        P(WIDE, "narrow", None),
        P((*WIDE, "narrow"), None),
    )
    return jax.shard_map(
        body,
        mesh=split,
        in_specs=placed,
        out_specs=(P(WIDE, "narrow", None), P(WIDE, "narrow", None)),
        check_vma=False,
    )
```

```python
import jax
import jax.numpy as jnp
from jax import lax
from jax.experimental import pallas as pl
from jax.experimental.pallas import tpu as pltpu
from jax.sharding import Mesh
from jax.sharding import PartitionSpec as P


BLOCK = 8
SWEEPS = 4
CX = 16
CY = 16
NZ = 128
MATERIALS = 16
NEAR = 0.5 / 16
FAR = 15.5 / 16
INTERPRET = False
GRANT = 8 * 1024 * 1024
EXACT = lax.Precision.HIGHEST
F32 = jnp.float32
WIDE = ("half", "plane")
SHIFTS = [(i, j) for i in range(4) for j in range(4) if i in (1, 2) or j in (1, 2)]

VMEM = pl.BlockSpec(memory_space=pltpu.VMEM)
SMEM = pl.BlockSpec(memory_space=pltpu.SMEM)


def row_at(i):
    return (i + 0.5) / CX


def iota(shape, axis):
    return lax.broadcasted_iota(jnp.int32, shape, axis)


def rolled(value, shift, axis):
    return pltpu.roll(value, shift % value.shape[axis], axis)


def place():
    planes, narrow = lax.axis_size("plane"), lax.axis_index("narrow")
    wide = lax.axis_index("half") * planes + lax.axis_index("plane")
    last_wide, last_narrow = lax.axis_size("half") * planes - 1, lax.axis_size("narrow") - 1
    inside = tuple(
        jnp.where(flag, F32(1.0), F32(0.0))
        for flag in (wide > 0, wide < last_wide, narrow > 0, narrow < last_narrow)
    )
    return wide % 2 == 0, narrow % 2 == 0, inside


def sided(even, first, second):
    return jnp.where(even, second, first), jnp.where(even, first, second)


def eta_pair():
    eta = (iota((CY, NZ), 0).astype(F32) + 0.5) / CY
    return 1.0 - eta, eta


def robin_of(robin_index, robin_table):
    return robin_table[robin_index[0]], robin_table[robin_index[1]]


class Coefficients:
    def __init__(self, kap):
        row = lambda r: jnp.broadcast_to(kap[r : r + 1, :], (BLOCK, NZ))
        tile = lambda low, high: jnp.concatenate([row(low), row(high)], 0)
        at_y, at_z = iota((CY, NZ), 0), iota((CY, NZ), 1)
        both = (tile(0, 1), tile(2, 3))
        self.x = (
            [0.5 * (both[0] + tile(4, 5))]
            + [both[0]] * 7
            + [0.5 * (both[0] + both[1])]
            + [both[1]] * 7
            + [0.5 * (both[1] + tile(6, 7))]
        )
        self.south, self.north, self.below, self.above = [], [], [], []
        self.rest = []
        for a in range(2):
            k = both[a]
            flipped = tile(2 * a + 1, 2 * a)
            middle = 0.5 * (k + flipped)
            south = jnp.where(at_y == 0, 0.5 * (k + tile(8 + a, 8 + a)), jnp.where(at_y == BLOCK, middle, k))
            north = jnp.where(
                at_y == CY - 1, 0.5 * (k + tile(10 + a, 10 + a)), jnp.where(at_y == BLOCK - 1, middle, k)
            )
            below = jnp.where(at_z == 0, k, 0.5 * (k + rolled(k, 1, 1)))
            above = jnp.where(at_z == NZ - 1, k, 0.5 * (k + rolled(k, -1, 1)))
            self.south.append(south)
            self.north.append(north)
            self.rest.append(south + north + below + above)
            self.below.append(jnp.where(at_z == 0, 0.0, below))
            self.above.append(jnp.where(at_z == NZ - 1, 0.0, above))
        self.south_in = [jnp.where(at_y == 0, 0.0, c) for c in self.south]
        self.north_in = [jnp.where(at_y == CY - 1, 0.0, c) for c in self.north]
        self.at_y = at_y
        self.totals = {}

    def total(self, i):
        key = i if i in (0, 7, 8, 15) else i // BLOCK + 20
        if key not in self.totals:
            self.totals[key] = 1.0 + self.x[i] + self.x[i + 1] + self.rest[i // BLOCK]
        return self.totals[key]

    def coupling(self, u, i):
        a, here = i // BLOCK, u[i]
        total = self.south_in[a] * rolled(here, 1, 0) + self.north_in[a] * rolled(here, -1, 0)
        total = total + self.below[a] * rolled(here, 1, 1) + self.above[a] * rolled(here, -1, 1)
        if i > 0:
            total = total + self.x[i] * u[i - 1]
        if i < CX - 1:
            total = total + self.x[i + 1] * u[i + 1]
        return total


def relax(coef, inside, robin, u, source, first):
    at_y = coef.at_y
    side_y = robin[1] * (
        jnp.where(at_y == 0, inside[2], 0.0) + jnp.where(at_y == CY - 1, inside[3], 0.0)
    )
    inverse = {}
    for i in range(CX):
        key = i if i in (0, 7, 8, 15) else i // BLOCK + 20
        if key not in inverse:
            diagonal = coef.total(i) + side_y
            if i == 0:
                diagonal = diagonal + robin[0] * inside[0]
            if i == CX - 1:
                diagonal = diagonal + robin[0] * inside[1]
            inverse[key] = 1.0 / diagonal
        inverse[i + 100] = inverse[key]
    odd = (iota((CY, NZ), 0) + iota((CY, NZ), 1)) % 2
    masks = (odd == 0, odd == 1)
    for half in range(2 * SWEEPS):
        for i in range(CX):
            mask = masks[(i + half) % 2]
            if first and half == 0:
                u[i] = jnp.where(mask, source[i] * inverse[i + 100], 0.0)
            else:
                update = (source[i] + coef.coupling(u, i)) * inverse[i + 100]
                u[i] = jnp.where(mask, update, u[i])


def contribute(coef, inside, u, right, sums, out):
    weights = eta_pair()
    zero = jnp.zeros((CY, NZ), F32)
    own, south, north = [zero, zero], [zero, zero], [zero, zero]
    for i in range(CX):
        a, here = i // BLOCK, u[i]
        left = right[i] - coef.total(i) * here + coef.coupling(u, i)
        low, high = coef.south[a] * here, coef.north[a] * here
        for side, weight in enumerate((1.0 - row_at(i), row_at(i))):
            own[side] = own[side] + weight * left
            south[side] = south[side] + weight * low
            north[side] = north[side] + weight * high
    across = lambda value, b: jnp.sum(value * weights[b], axis=0, keepdims=True)
    west, east = inside[0] * coef.x[0] * u[0], inside[1] * coef.x[CX] * u[CX - 1]
    west_row = [across(west, b) for b in range(2)]
    east_row = [across(east, b) for b in range(2)]
    south_row = [inside[2] * south[a][:1] for a in range(2)]
    north_row = [inside[3] * north[a][CY - 1 :] for a in range(2)]
    sums[...] = jnp.zeros_like(sums)
    for a in range(2):
        for b in range(2):
            near_x, near_y = (west_row, east_row)[a][b], (south_row, north_row)[b][a]
            at = (1 + a) * 4 + 1 + b
            sums[at : at + 1, :] = across(own[a], b) + FAR * (near_x + near_y)
    for b in range(2):
        sums[1 + b : 2 + b, :] = NEAR * west_row[b]
        sums[13 + b : 14 + b, :] = NEAR * east_row[b]
    for a in range(2):
        at = (1 + a) * 4
        sums[at : at + 1, :] = NEAR * south_row[a]
        sums[at + 3 : at + 4, :] = NEAR * north_row[a]
    column = jnp.sum(sums[...], axis=1, keepdims=True)
    spread = jnp.where(iota((16, NZ), 0) == iota((16, NZ), 1) % 16, column, 0.0)
    out[...] = jnp.broadcast_to(jnp.sum(spread, axis=0, keepdims=True), out.shape)


def pack_kernel(labels, row, pay):
    pay[...] = jnp.zeros_like(pay)
    for a in range(2):
        pay[2 * a : 2 * a + 2, 0 : labels.shape[2]] = labels[a].astype(F32)
    for c in range(row.shape[1] // NZ):
        pay[4 + c : 5 + c, :] = row[:, c * NZ : (c + 1) * NZ]


def first_kernel(right, table, robin_table, robin_index, own, y2, y1, x1, x2, u, out, kap, fx2, fx1, fy1, fy2, sums):
    even_x, even_y, inside = place()
    from_west, from_east = sided(even_x, x1[...], x2[...])
    from_south, from_north = sided(even_y, y1[...], y2[...])
    keys = jnp.concatenate([own[...], from_west, from_east, from_south, from_north], 0)
    pick = (iota((NZ, NZ), 0) == iota((NZ, NZ), 1) // BLOCK).astype(F32)
    keys = jnp.dot(keys, pick, preferred_element_type=F32)
    found = jnp.zeros_like(keys)
    for m in range(MATERIALS):
        found = jnp.where(jnp.abs(keys - m) < 0.5, table[m], found)
    kap[...] = jnp.zeros_like(kap)
    kap[0:4, :] = found[0:4]
    for b in range(2):
        own_of = lambda a, c: found[2 * a + c : 2 * a + c + 1]
        kap[4 + b : 5 + b, :] = jnp.where(inside[0] > 0, found[10 + b : 11 + b], own_of(0, b))
        kap[6 + b : 7 + b, :] = jnp.where(inside[1] > 0, found[16 + b : 17 + b], own_of(1, b))
        kap[8 + b : 9 + b, :] = jnp.where(inside[2] > 0, found[25 + 2 * b : 26 + 2 * b], own_of(b, 0))
        kap[10 + b : 11 + b, :] = jnp.where(inside[3] > 0, found[32 + 2 * b : 33 + 2 * b], own_of(b, 1))
    coef = Coefficients(kap)
    relax(coef, inside, robin_of(robin_index, robin_table), u, right, True)
    contribute(coef, inside, u, right, sums, out)
    faces(even_x, even_y, u, (fx2, fx1, fy1, fy2))


def faces(even_x, even_y, u, sends):
    sx2, sx1, sy1, sy2 = sends
    for i in range(CX):
        south, north = u[i][:1], u[i][CY - 1 :]
        sy1[i : i + 1, :] = jnp.where(even_y, north, south)
        sy2[i : i + 1, :] = jnp.where(even_y, south, north)
    sx1[0:CY, :] = jnp.where(even_x, u[CX - 1], u[0])
    sx2[0:CY, :] = jnp.where(even_x, u[0], u[CX - 1])


def put_rows(out, face, pieces):
    out[0:CX, :] = face[...]
    for k, piece in enumerate((*pieces, jnp.zeros((4, NZ), F32))):
        out[CX + 4 * k : CX + 4 * k + 4, :] = piece


def taken(value, k):
    return value[CX + 4 * k : CX + 4 * k + 4]


def ride_x_kernel(x2, x1, y1, y2, fx2, fx1, px2, px1):
    even_x, even_y, _ = place()
    east = sided(even_x, x1[...], x2[...])[1][4:8]
    south, north = (p[4:8] for p in sided(even_y, y1[...], y2[...]))
    for out, face in ((px2, fx2), (px1, fx1)):
        put_rows(out, face, (east, north, south))


def ride_y_kernel(y1, y2, q2, q1, fy1, fy2, py1, py2):
    even_x, even_y, _ = place()
    north = sided(even_y, y1[...], y2[...])[1][4:8]
    beyond = sided(even_x, q1[...], q2[...])[1]
    for out, face in ((py1, fy1), (py2, fy2)):
        put_rows(out, face, (north, taken(beyond, 0), taken(beyond, 1)))


def widen_kernel(own, x2, x1, y1, y2, q2, q1, r1, r2, shifted, rows, moves):
    even_x, even_y, _ = place()
    count = rows.shape[1]
    narrow_count = lax.axis_size("narrow")
    wide_count = count // narrow_count
    west, east = (p[4:8] for p in sided(even_x, x1[...], x2[...]))
    south, north = (p[4:8] for p in sided(even_y, y1[...], y2[...]))
    before, beyond = sided(even_x, q1[...], q2[...])
    above = sided(even_y, r1[...], r2[...])[1]
    held = (
        own[4:8], east, north, taken(beyond, 1),
        west, taken(before, 1),
        taken(beyond, 0), taken(above, 1),
        south, taken(beyond, 2),
        taken(above, 0), taken(above, 2),
    )
    rows[...] = jnp.zeros_like(rows)
    for k, piece in enumerate(held):
        for c in range(count // NZ):
            rows[k : k + 1, c * NZ : (c + 1) * NZ] = piece[c : c + 1]
    at = iota((16, count), 1)
    at_x, at_y = at // narrow_count, at % narrow_count
    value = rows[...]
    for t, (i, j) in enumerate(SHIFTS):
        x, y = at_x + (i - 1), at_y + (j - 1)
        fits = (x >= 0) & (x < wide_count) & (y >= 0) & (y < narrow_count)
        moved = rolled(value, -((i - 1) * narrow_count + j - 1), 1)
        moves[16 * t : 16 * t + 16, :] = jnp.where(fits, moved, 0.0)
    planes = lax.axis_size("plane")
    source, target = iota((count, count), 0), iota((count, count), 1)
    half, plane = target // (narrow_count * planes), target % planes
    wanted = (half * planes + plane) * narrow_count + target // planes % narrow_count
    order = (source == wanted).astype(F32)
    shifted[...] = jnp.dot(moves[...], order, precision=EXACT, preferred_element_type=F32)


def turn_kernel(arrived, out):
    groups = arrived.shape[0] // 8
    mine = iota((8, NZ), 1) // 16 == iota((8, NZ), 0)
    rows = []
    for q in range(groups):
        kept = jnp.where(mine, arrived[8 * q : 8 * q + 8, :], 0.0)
        rows.append(jnp.sum(kept, axis=0, keepdims=True))
    tile = jnp.concatenate(rows * (8 // groups), 0)
    for b in range(out.shape[0] // 8):
        out[8 * b : 8 * b + 8, :] = tile


def window(every, shifted, opened):
    mine = iota((8, NZ), 1) // 16 == iota((8, NZ), 0)
    for d in range(every.shape[0]):
        row = jnp.broadcast_to(every[d : d + 1, :], (8, NZ))
        opened[8 * d : 8 * d + 8, :] = jnp.where(mine, row, 0.0)
    product = jnp.dot(shifted[...], opened[...], precision=EXACT, preferred_element_type=F32)
    lane = iota((16, NZ), 1) % 16
    picked = jnp.zeros((16, NZ), F32)
    for t, (i, j) in enumerate(SHIFTS):
        picked = picked + jnp.where(lane == 4 * i + j, product[16 * t : 16 * t + 16], 0.0)
    value = jnp.sum(picked, axis=1, keepdims=True)
    return [jnp.broadcast_to(value[k : k + 1], (CY, NZ)) for k in range(12)]


def correct(even_x, even_y, value, old, new, seen):
    low, high = eta_pair()
    v00, v10, v01, v11, w0, w1, e0, e1, s0, s1, n0, n1 = value
    ramp = lambda first, second: first * low + second * high
    west, east, south, north = ramp(v00, v01), ramp(v10, v11), ramp(v00, v10), ramp(v01, v11)
    for i in range(CX):
        new[i] = old[i] + ((1.0 - row_at(i)) * west + row_at(i) * east)
    seen_x = sided(even_x, seen[1][0:CY], seen[0][0:CY])
    seen_y = sided(even_y, seen[2][0:CX], seen[3][0:CX])
    return (
        seen_x[0] + (NEAR * ramp(w0, w1) + FAR * west),
        seen_x[1] + (FAR * east + NEAR * ramp(e0, e1)),
        seen_y[0] + (NEAR * ramp(s0, s1) + FAR * south),
        seen_y[1] + (FAR * north + NEAR * ramp(n0, n1)),
    )


def second_kernel(
    right, robin_table, robin_index, kap, old, every, shifted, q2, q1, r1, r2,
    u, out, fx2, fx1, fy1, fy2, source, sums, opened,
):
    even_x, even_y, inside = place()
    seen = (q2, q1, r1, r2)
    value = window(every, shifted, opened)
    west, east, south, north = correct(even_x, even_y, value, old, u, seen)
    robin = robin_of(robin_index, robin_table)
    coef = Coefficients(kap)
    for i in range(CX):
        a, here = i // BLOCK, u[i]
        total = right[i]
        trace = inside[2] * (coef.south[a] * south[i : i + 1] + robin[1] * here)
        total = total + jnp.where(coef.at_y == 0, trace, 0.0)
        trace = inside[3] * (coef.north[a] * north[i : i + 1] + robin[1] * here)
        total = total + jnp.where(coef.at_y == CY - 1, trace, 0.0)
        if i == 0:
            total = total + inside[0] * (coef.x[0] * west + robin[0] * here)
        if i == CX - 1:
            total = total + inside[1] * (coef.x[CX] * east + robin[0] * here)
        source[i] = total
    relax(coef, inside, robin, u, source, False)
    contribute(coef, inside, u, right, sums, out)
    faces(even_x, even_y, u, (fx2, fx1, fy1, fy2))


def last_kernel(right, kap, old, every, shifted, q2, q1, r1, r2, answer, out, u, opened):
    even_x, even_y, inside = place()
    value = window(every, shifted, opened)
    west, east, south, north = correct(even_x, even_y, value, old, u, (q2, q1, r1, r2))
    coef = Coefficients(kap)
    for i in range(CX):
        a = i // BLOCK
        left = right[i] - coef.total(i) * u[i] + coef.coupling(u, i)
        left = left + jnp.where(coef.at_y == 0, inside[2] * coef.south[a] * south[i : i + 1], 0.0)
        left = left + jnp.where(coef.at_y == CY - 1, inside[3] * coef.north[a] * north[i : i + 1], 0.0)
        if i == 0:
            left = left + inside[0] * coef.x[0] * west
        if i == CX - 1:
            left = left + inside[1] * coef.x[CX] * east
        out[i] = left.astype(jnp.bfloat16)
        answer[i] = u[i].astype(jnp.bfloat16)


def call(kernel, out_shape, spaces, scratch=()):
    return pl.pallas_call(
        kernel,
        out_shape=out_shape,
        in_specs=list(spaces),
        out_specs=jax.tree.map(lambda _: VMEM, out_shape),
        scratch_shapes=list(scratch),
        interpret=INTERPRET,
        compiler_params=pltpu.CompilerParams(vmem_limit_bytes=GRANT),
    )


def swap_pairs(peers, start):
    pairs = []
    for i in range(start, peers - 1, 2):
        pairs += [(i, i + 1), (i + 1, i)]
    return pairs


def swap(array, axis, start):
    return lax.ppermute(array, axis, swap_pairs(lax.axis_size(axis), start))


def swaps(sx2, sx1, sy1, sy2):
    x2 = swap(sx2, WIDE, 1)
    x1 = swap(sx1, WIDE, 0)
    y1 = swap(sy1, "narrow", 0)
    y2 = swap(sy2, "narrow", 1)
    return x2, x1, y1, y2


def gather_plane(values):
    return lax.all_to_all(values, "plane", 0, 0, tiled=True)


def gather_line(near, count):
    turned = call(turn_kernel, jax.ShapeDtypeStruct((count // 8, NZ), F32), [VMEM])(near)
    return lax.all_to_all(turned, ("half", "narrow"), 0, 0, tiled=True)


def body(right_side, labels, material_table, robin_table, robin_index, coarse_rows):
    count = coarse_rows.shape[1]
    shape = lambda *dims: jax.ShapeDtypeStruct(dims, F32)
    scratch = lambda *dims: pltpu.VMEM(dims, F32)
    field, face, mine = shape(CX, CY, NZ), shape(CY, NZ), shape(lax.axis_size("plane"), NZ)
    index = robin_index[0, 0]
    pay = call(pack_kernel, shape(8, NZ), [VMEM] * 2)(labels, coarse_rows)
    x2, x1, y1, y2 = swaps(pay, pay, pay, pay)
    u, sent, kap, fx2, fx1, fy1, fy2 = call(
        first_kernel,
        (field, mine, shape(16, NZ), face, face, face, face),
        [VMEM] + [SMEM] * 3 + [VMEM] * 5,
        [scratch(16, NZ)],
    )(right_side, material_table, robin_table, index, pay, y2, y1, x1, x2)
    near = gather_plane(sent)
    ridden, lines = (shape(CX + 16, NZ),) * 2, 16 * len(SHIFTS)
    px2, px1 = call(ride_x_kernel, ridden, [VMEM] * 6)(x2, x1, y1, y2, fx2, fx1)
    q2, q1 = swap(px2, WIDE, 1), swap(px1, WIDE, 0)
    every = gather_line(near, count)
    py1, py2 = call(ride_y_kernel, ridden, [VMEM] * 6)(y1, y2, q2, q1, fy1, fy2)
    seen = (q2, q1, swap(py1, "narrow", 0), swap(py2, "narrow", 1))
    shifted = call(
        widen_kernel, shape(lines, count), [VMEM] * 9, [scratch(16, count), scratch(lines, count)]
    )(pay, x2, x1, y1, y2, *seen)
    u, sent, *edges = call(
        second_kernel,
        (field, mine, face, face, face, face),
        [VMEM] + [SMEM] * 2 + [VMEM] * 8,
        [scratch(CX, CY, NZ), scratch(16, NZ), scratch(count, NZ)],
    )(right_side, robin_table, index, kap, u, every, shifted, *seen)
    near = gather_plane(sent)
    every = gather_line(near, count)
    seen = swaps(*edges)
    half = jax.ShapeDtypeStruct((CX, CY, NZ), jnp.bfloat16)
    return call(last_kernel, (half, half), [VMEM] * 9, [scratch(CX, CY, NZ), scratch(count, NZ)])(
        right_side, kap, u, every, shifted, *seen
    )


def solution(mesh):
    devices = mesh.devices
    split = Mesh(devices.reshape(2, devices.shape[0] // 2, -1), (*WIDE, "narrow"))
    placed = (
        P(WIDE, "narrow", None),
        P(WIDE, "narrow", None),
        P(),
        P(),
        P(WIDE, "narrow", None),
        P((*WIDE, "narrow"), None),
    )
    return jax.shard_map(
        body,
        mesh=split,
        in_specs=placed,
        out_specs=(P(WIDE, "narrow", None), P(WIDE, "narrow", None)),
        check_vma=False,
    )
```
